32 devices in a mesh: rep: 4 (over x, core), shard: 8 (over z, y).
Axes of the slice: x: 2, y: 2, z: 4, core: 2. Of those that a mesh axis runs over, the one named last changes fastest.
Arguments:
- tokens: bfloat16 [4096, 2304], P(('rep', 'shard')), may hold values from -6 to 6
- doc_lengths: int32 [32, 2], P(('rep', 'shard')), may hold values from 1 to 96, 128 in all within a row
- pic_starts: int32 [32, 2], P(('rep', 'shard')), may hold values from 0 to 64
- attn_gain: float32 [2304], P('shard'), may hold values from 0.5 to 1.5
- w_query: float32 [2304, 2304], P('shard'), may hold values from -0.125 to 0.125
- w_key: float32 [2304, 2304], P('shard'), may hold values from -0.125 to 0.125
- w_value: float32 [2304, 2304], P('shard'), may hold values from -0.125 to 0.125
- w_out: float32 [2304, 2304], P('shard'), may hold values from -3.6 to 3.6
- ffn_gain: float32 [2304], P('shard'), may hold values from 0.5 to 1.5
- w_gate: float32 [2304, 5760], P('shard'), may hold values from -0.125 to 0.125
- w_up: float32 [2304, 5760], P('shard'), may hold values from -0.125 to 0.125
- w_down: float32 [5760, 2304], P('shard'), may hold values from -0.6 to 0.6
- cotangent: bfloat16 [4096, 2304], P(('rep', 'shard')), may hold values from -6 to 6
Outputs:
- out_tokens: bfloat16 [4096, 2304], P(('rep', 'shard'))
- input_grad: float32 [4096, 2304], P(('rep', 'shard'))
- attn_gain_grad: float32 [2304], P('shard')
- query_grad: float32 [2304, 2304], P('shard')
- key_grad: float32 [2304, 2304], P('shard')
- value_grad: float32 [2304, 2304], P('shard')
- out_grad: float32 [2304, 2304], P('shard')
- ffn_gain_grad: float32 [2304], P('shard')
- gate_grad: float32 [2304, 5760], P('shard')
- up_grad: float32 [2304, 5760], P('shard')
- down_grad: float32 [5760, 2304], P('shard')
The draws below stay inside these ranges and needn't reach their ends.
Inputs may be any that keep to these rules, and one draw needn't show every extreme that they name: `doc_lengths`: each row of 2 lengths sums to 128. `pic_starts`: pieces may intersect each other and cross document ends.
All inputs are finite; a program needn't handle non-finite values.
Results may differ from the reference program's by a relative error of at most 0.02.
Values may be sent and summed in bfloat16 or wider, within the bound.
No kernel may reach another device: no remote copies, remote signals or barrier semaphores. Data moves between devices by JAX's collectives and lax.ppermute only.
A program may use at most 512 MiB of HBM per device.

```python
import math
from functools import partial
import jax
import jax.numpy as jnp
import numpy as np
from jax import lax

D = 2304
H = 36
HD = 64
FF = 5760
TOK_DEV = 128
DOCS = 2
PICS = 2
PIC = 64
TOKENS = 4096
DEVICES = 32


def plant(entries, key, least, high):
    extent = entries.shape
    place = [jax.random.randint(jax.random.fold_in(key, axis), (), 0, extent[axis]) for axis in range(len(extent))]
    entries = entries.at[tuple(place)].set(least)
    longest = extent.index(max(extent))
    place[longest] = (place[longest] + 1) % extent[longest]
    return entries.at[tuple(place)].set(high)


def block_levels(rng, extent, split, least, high):
    def one(position, parts):
        draws = jax.random.uniform(jax.random.fold_in(jax.random.fold_in(rng, 6), position), (parts,), jnp.float32, least / len(split), high / len(split))
        return jnp.repeat(jnp.exp(draws), extent[position] // parts).reshape((-1,) + (1,) * (len(extent) - position - 1))

    factor_of = one(*split[0])
    for cut in split[1:]:
        factor_of = factor_of * one(*cut)
    return factor_of


def profile(number_of, total, reach, skew):
    loads = [(1 << 20) // math.isqrt(rank ** skew) + 1 for rank in range(2, number_of + 1)]
    rest, holding = total - reach - (number_of - 1), [1] * (number_of - 1)
    while rest > 0:
        movable = [i for i in range(number_of - 1) if holding[i] < reach]
        whole, left = sum([loads[i] for i in movable]), rest
        for i in movable:
            more = min(reach - holding[i], max(1, left * loads[i] // whole), rest)
            holding[i] = holding[i] + more
            rest = rest - more
    return np.array([reach] + holding)


def uneven(key, amount, total, bound, lean):
    if amount == 2:
        one = jax.random.randint(key, (), max(1, total - bound), min(bound, total - 1) + 1)
        return jnp.stack([one, total - one])
    sizes = jnp.asarray(profile(amount, total, bound, lean), jnp.int32)
    twos = (amount - 1) // 2
    donor, sink = sizes[1:1 + 2 * twos:2], sizes[2:2 + 2 * twos:2]
    room = jnp.minimum(donor - 1, bound - sink)
    moved = jax.random.randint(jax.random.fold_in(key, 1), (twos,), 0, 1 << 20) % (room + 1)
    sizes = sizes.at[1:1 + 2 * twos:2].set(donor - moved).at[2:2 + 2 * twos:2].set(sink + moved)
    return sizes[jax.random.permutation(jax.random.fold_in(key, 2), amount)]


def bell_draw(stream_key, shape, deviation, bound, split=(), kind=jnp.bfloat16):
    drawn = deviation * jax.random.normal(stream_key, shape, jnp.float32)
    if split:
        drawn = drawn * block_levels(stream_key, shape, split, -0.22, 0.18)
    return jnp.clip(drawn, -bound, bound).astype(kind)


def setup_inputs(seed: int = 0) -> dict:
    key_list = jax.random.split(jax.random.key(seed), 14)
    return {
        "tokens": bell_draw(key_list[0], (TOKENS, D), 1.0, 6.0, ((0, 32),)),
        "doc_lengths": jax.vmap(lambda own: uneven(own, DOCS, TOK_DEV, TOK_DEV * 3 // 4, 0))(jax.random.split(key_list[1], DEVICES)).reshape((DEVICES, DOCS)).astype(jnp.int32),
        "pic_starts": plant(jax.random.randint(key_list[2], (DEVICES, PICS), 0, TOK_DEV - PIC + 1), jax.random.fold_in(key_list[2], 1), 0, TOK_DEV - PIC).astype(jnp.int32),
        "attn_gain": jnp.clip(1.0 + 0.1 * jax.random.normal(key_list[3], (D,), jnp.float32), 0.5, 1.5),
        "w_query": bell_draw(key_list[4], (D, D), D ** -0.5, 0.125, ((0, 8),), jnp.float32),
        "w_key": bell_draw(key_list[5], (D, D), D ** -0.5, 0.125, ((0, 8),), jnp.float32),
        "w_value": bell_draw(key_list[6], (D, D), D ** -0.5, 0.125, ((0, 8),), jnp.float32),
        "w_out": bell_draw(key_list[7], (D, D), 0.6, 3.6, ((0, 8),), jnp.float32),
        "ffn_gain": jnp.clip(1.0 + 0.1 * jax.random.normal(key_list[8], (D,), jnp.float32), 0.5, 1.5),
        "w_gate": bell_draw(key_list[9], (D, FF), D ** -0.5, 0.125, ((0, 8),), jnp.float32),
        "w_up": bell_draw(key_list[10], (D, FF), D ** -0.5, 0.125, ((0, 8),), jnp.float32),
        "w_down": bell_draw(key_list[11], (FF, D), 0.1, 0.6, ((0, 8),), jnp.float32),
        "cotangent": bell_draw(key_list[12], (TOKENS, D), 1.0, 6.0, ((0, 32),)),
    }


EPSILON = 1e-05
BRANCH_SCALE = 1.4 / math.sqrt(40.0)
MASKED = -1e+30
HIGH = lax.Precision.HIGHEST

@jax.custom_vjp
def low(v):
    return lax.optimization_barrier(v.astype(jnp.bfloat16)).astype(jnp.float32)

@jax.custom_vjp
def low_back(v):
    return v

def low_keep(v):
    return (low(v), None)

def low_pass(kept, grad):
    return (grad,)

def back_keep(v):
    return (v, None)

def back_low(kept, grad):
    return (low(grad),)
low.defvjp(low_keep, low_pass)
low_back.defvjp(back_keep, back_low)

def layout(lengths, starts, row_count):
    places = jnp.arange(row_count, dtype=jnp.int32)
    bounds = jnp.cumsum(lengths).astype(jnp.int32)
    firsts = bounds - lengths
    member = (places[:, None] >= firsts[None, :]) & (places[:, None] < bounds[None, :])
    doc_of = lax.optimization_barrier(jnp.sum(jnp.where(member, jnp.arange(lengths.shape[0], dtype=jnp.int32)[None, :], 0), axis=1))
    starting = lax.optimization_barrier(jnp.sum(jnp.where(member, firsts[None, :], 0), axis=1))
    inside = (places[None, :] >= starts[:, None]) & (places[None, :] < starts[:, None] + PIC)
    shared = jnp.any(inside[:, :, None] & inside[:, None, :], axis=0)
    causal = places[None, :] <= places[:, None]
    allowed = (doc_of[:, None] == doc_of[None, :]) & (causal | shared)
    return ((places - starting).astype(jnp.int32), allowed.astype(jnp.int32))

def angles(offsets, head_size):
    half_size = head_size // 2
    freq_table = jnp.exp(jnp.arange(half_size, dtype=jnp.float32) * (-2.0 * math.log(10000.0) / head_size))
    turned = offsets.astype(jnp.float32)[:, None] * freq_table[None, :]
    return (jnp.cos(turned)[:, None, :], jnp.sin(turned)[:, None, :])

def rotate(values, cosine, sine):
    half_size = values.shape[-1] // 2
    first_half = values[..., :half_size]
    second_half = values[..., half_size:]
    return jnp.concatenate([first_half * cosine - second_half * sine, second_half * cosine + first_half * sine], axis=-1)

def matmul(left, right):
    return jnp.dot(left, right, precision=HIGH, preferred_element_type=jnp.float32)

def attend(blocks):
    query, keys, values, allowed = blocks
    scores = jnp.einsum('qhd,khd->hqk', query, keys, precision=HIGH) * HD ** (-0.5)
    scores = low_back(scores)
    scores = jnp.where(allowed[None] != 0, scores, MASKED)
    highest = lax.optimization_barrier(jnp.max(scores, axis=-1, keepdims=True))
    expo = jnp.exp(scores - highest)
    probs = low(expo / lax.optimization_barrier(jnp.sum(expo, axis=-1, keepdims=True)))
    return jnp.einsum('hqk,khd->qhd', probs, values, precision=HIGH)

def reference(tokens, doc_lengths, pic_starts, attn_gain, w_query, w_key, w_value, w_out, ffn_gain, w_gate, w_up, w_down, cotangent):
    offsets, allowed = jax.vmap(partial(layout, row_count=TOK_DEV))(doc_lengths, pic_starts)
    cosine, sine = angles(offsets.reshape(TOKENS), HD)

    def forward(inputs, gain_one, query_w, key_w, value_w, out_w, gain_two, gate_w, up_w, down_w):
        scale_one = lax.rsqrt(lax.optimization_barrier(jnp.mean(inputs * inputs, axis=-1, keepdims=True)) + EPSILON)
        hidden_one = low(inputs * scale_one * low(gain_one))
        query = low(rotate(low_back(matmul(hidden_one, low(query_w))).reshape(TOKENS, H, HD), cosine, sine))
        keys = low(rotate(low_back(matmul(hidden_one, low(key_w))).reshape(TOKENS, H, HD), cosine, sine))
        values = low(low_back(matmul(hidden_one, low(value_w))))
        mixed = lax.map(jax.checkpoint(attend), (query.reshape(DEVICES, TOK_DEV, H, HD), keys.reshape(DEVICES, TOK_DEV, H, HD), values.reshape(DEVICES, TOK_DEV, H, HD), allowed))
        mixed = low(low_back(mixed.reshape(TOKENS, D)))
        middle = inputs + BRANCH_SCALE * low_back(matmul(mixed, low(out_w)))
        scale_two = lax.rsqrt(lax.optimization_barrier(jnp.mean(middle * middle, axis=-1, keepdims=True)) + EPSILON)
        hidden_two = low(middle * scale_two * low(gain_two))
        gate_act = low_back(matmul(hidden_two, low(gate_w)))
        up_act = low_back(matmul(hidden_two, low(up_w)))
        inner = low(jax.nn.silu(gate_act) * up_act)
        return middle + BRANCH_SCALE * low_back(matmul(inner, low(down_w)))
    inputs = tokens.astype(jnp.float32)
    result, pullback = jax.vjp(forward, inputs, attn_gain, w_query, w_key, w_value, w_out, ffn_gain, w_gate, w_up, w_down)
    grads = pullback(cotangent.astype(jnp.float32))
    return (result.astype(jnp.bfloat16), grads[0], grads[1], grads[2], grads[3], grads[4], grads[5], grads[6], grads[7], grads[8], grads[9])
```

```python
import math

import jax
import jax.numpy as jnp
from jax import lax
from jax.sharding import PartitionSpec as P

HD = 64
PIC = 64

EPSILON = 1e-05
BRANCH_SCALE = 1.4 / math.sqrt(40.0)
MASKED = -1e30
F32 = jnp.float32
BF16 = jnp.bfloat16


def mm(left, right, contract):
    return lax.dot_general(left, right, ((contract[0], contract[1]), ((), ())), preferred_element_type=F32)


def layout(lengths, starts, row_count):
    places = jnp.arange(row_count, dtype=jnp.int32)
    bounds = jnp.cumsum(lengths)
    firsts = bounds - lengths
    member = (places[:, None] >= firsts[None, :]) & (places[:, None] < bounds[None, :])
    doc_of = jnp.sum(
        jnp.where(member, jnp.arange(lengths.shape[0], dtype=jnp.int32)[None, :], 0), axis=1
    )
    starting = jnp.sum(jnp.where(member, firsts[None, :], 0), axis=1)
    inside = (places[None, :] >= starts[:, None]) & (places[None, :] < starts[:, None] + PIC)
    shared = jnp.any(inside[:, :, None] & inside[:, None, :], axis=0)
    causal = places[None, :] <= places[:, None]
    allowed = (doc_of[:, None] == doc_of[None, :]) & (causal | shared)
    return (places - starting, allowed)


def angles(offsets, head_size):
    half_size = head_size // 2
    freq_table = jnp.exp(
        jnp.arange(half_size, dtype=F32) * (-2.0 * math.log(10000.0) / head_size)
    )
    turned = offsets.astype(F32)[..., None] * freq_table
    return jnp.cos(turned)[:, :, None, :], jnp.sin(turned)[:, :, None, :]


def rotate(values, cosine, sine):
    half_size = values.shape[-1] // 2
    first_half = values[..., :half_size]
    second_half = values[..., half_size:]
    return jnp.concatenate(
        [first_half * cosine - second_half * sine, second_half * cosine + first_half * sine],
        axis=-1,
    )


def build(rep, shard):
    n = shard

    def gather_shard(piece):
        return lax.all_gather(piece, "shard", axis=0, tiled=True)

    def scatter_shard(whole):
        return lax.psum_scatter(whole, "shard", scatter_dimension=0, tiled=True)

    def exchange(blocks):
        return lax.all_to_all(blocks, "shard", split_axis=0, concat_axis=0, tiled=True)

    def gather_rep(piece):
        return lax.all_gather(piece, "rep", axis=0, tiled=False)

    def scatter_rep(whole):
        return lax.psum_scatter(whole, "rep", scatter_dimension=0, tiled=False)

    def local(
        tokens,
        doc_lengths,
        pic_starts,
        attn_gain,
        w_query,
        w_key,
        w_value,
        w_out,
        ffn_gain,
        w_gate,
        w_up,
        w_down,
        cotangent,
    ):
        rows, width = tokens.shape
        heads = width // HD
        slots = -(-heads // n)
        block = slots * HD
        spare = n * block - width
        depth = w_query.shape[0]
        part = depth // rep
        ff = w_gate.shape[1]
        cols = ff // n
        all_rows = n * rows
        me = lax.axis_index("shard")
        mine = lax.axis_index("rep")
        gain_one = attn_gain.astype(BF16).astype(F32)[:, None]
        gain_two = ffn_gain.astype(BF16).astype(F32)[:, None]

        def quarter(array):
            return lax.dynamic_slice_in_dim(array, mine * part, part, 0)

        def scaled(weight, gain):
            return (quarter(weight).astype(BF16).astype(F32) * quarter(gain)).astype(BF16)

        def head_blocks(weight):
            return jnp.pad(weight, ((0, 0), (0, spare))).reshape(weight.shape[0], n, block)

        qkv_part = jnp.concatenate(
            [head_blocks(scaled(w, gain_one)) for w in (w_query, w_key, w_value)], axis=2
        ).transpose(1, 0, 2)
        qkv_w = gather_rep(exchange(qkv_part)).transpose(1, 0, 2, 3).reshape(width, 3 * block)
        out_part = gather_shard(quarter(w_out).astype(BF16)).reshape(n, part, width)
        out_w = gather_rep(out_part).transpose(1, 0, 2, 3).reshape(width, width)
        out_w = jnp.pad(out_w, ((0, spare), (0, 0)))
        ffn_part = jnp.concatenate(
            [scaled(w, gain_two).reshape(part, n, cols) for w in (w_gate, w_up)], axis=2
        ).transpose(1, 0, 2)
        ffn_w = gather_rep(exchange(ffn_part)).transpose(1, 0, 2, 3).reshape(width, 2 * cols)
        down_w = w_down.astype(BF16)

        inputs = gather_shard(tokens).astype(F32)
        lengths = lax.all_gather(doc_lengths, "shard", axis=0, tiled=True)
        starts = lax.all_gather(pic_starts, "shard", axis=0, tiled=True)
        offsets, allowed = jax.vmap(lambda a, b: layout(a, b, rows))(lengths, starts)
        cosine, sine = angles(offsets, HD)
        scale_one = lax.rsqrt(jnp.mean(inputs * inputs, axis=-1, keepdims=True) + EPSILON)
        normed_one = (inputs * scale_one).astype(BF16)
        qkv = mm(normed_one, qkv_w, ((1,), (0,)))

        def split_heads(values):
            return values.reshape(n, rows, slots, HD)

        query = rotate(split_heads(qkv[:, :block]), cosine, sine).astype(BF16)
        keys = rotate(split_heads(qkv[:, block : 2 * block]), cosine, sine).astype(BF16)
        values = split_heads(qkv[:, 2 * block :].astype(BF16))
        scores = jnp.einsum("rqhd,rkhd->rhqk", query, keys, preferred_element_type=F32) * HD**-0.5
        scores = jnp.where(allowed[:, None], scores, MASKED)
        expo = jnp.exp(scores - jnp.max(scores, axis=-1, keepdims=True))
        probs = expo / jnp.sum(expo, axis=-1, keepdims=True)
        probs_low = probs.astype(BF16)
        mixed = jnp.einsum("rhqk,rkhd->rqhd", probs_low, values, preferred_element_type=F32)
        mixed = mixed.astype(BF16).reshape(all_rows, block)
        mixed_all = lax.all_gather(mixed, "shard", axis=0, tiled=False)
        mixed_all = mixed_all.transpose(1, 0, 2).reshape(all_rows, n * block)
        middle = inputs + BRANCH_SCALE * mm(mixed_all, out_w, ((1,), (0,)))

        scale_two = lax.rsqrt(jnp.mean(middle * middle, axis=-1, keepdims=True) + EPSILON)
        normed_two = (middle * scale_two).astype(BF16)
        both = mm(normed_two, ffn_w, ((1,), (0,)))
        gate_act = both[:, :cols]
        up_act = both[:, cols:]
        sigmoid_gate = jax.nn.sigmoid(gate_act)
        silu_gate = gate_act * sigmoid_gate
        inner = (silu_gate * up_act).astype(BF16)
        grad_result = cotangent.astype(F32)
        grad_branch = gather_shard((BRANCH_SCALE * grad_result).astype(BF16))
        grad_inner = mm(grad_branch, down_w, ((1,), (1,)))
        grad_gate_act = (
            grad_inner * up_act * sigmoid_gate * (1.0 + gate_act * (1.0 - sigmoid_gate))
        ).astype(BF16)
        grad_up_act = (grad_inner * silu_gate).astype(BF16)
        grad_both = jnp.concatenate([grad_gate_act, grad_up_act], axis=1)
        grad_normed_two = scatter_shard(mm(grad_both, ffn_w, ((1,), (1,))).astype(BF16)).astype(F32)
        my_middle = lax.dynamic_slice_in_dim(middle, me * rows, rows, 0)
        my_scale_two = lax.dynamic_slice_in_dim(scale_two, me * rows, rows, 0)
        my_normed_two = my_middle * my_scale_two
        inner_mean = jnp.mean(grad_normed_two * my_normed_two, axis=-1, keepdims=True)
        grad_middle = grad_result + my_scale_two * (grad_normed_two - my_normed_two * inner_mean)
        branch = scatter_shard(mm(inner, down_w, ((1,), (0,))).astype(BF16)).astype(F32)
        out_tokens = (my_middle + BRANCH_SCALE * branch).astype(BF16)

        def down_sum(grad):
            return lax.psum(grad.astype(BF16), "rep").astype(F32)

        def to_rows(grad):
            piece = grad.astype(BF16).reshape(n, rep, part, grad.shape[1]).transpose(1, 0, 2, 3)
            piece = gather_rep(exchange(scatter_rep(piece)))
            return piece.transpose(0, 2, 1, 3).reshape(depth, n, grad.shape[1]).astype(F32)

        grad_down = down_sum(mm(inner, grad_branch, ((0,), (0,))))
        grad_ffn = to_rows(mm(normed_two, grad_both, ((0,), (0,))))
        raw_gate = grad_ffn[:, :, :cols].reshape(depth, ff)
        raw_up = grad_ffn[:, :, cols:].reshape(depth, ff)

        def low(weight):
            return weight.astype(BF16).astype(F32)

        grad_gain_two = jnp.sum(low(w_gate) * raw_gate + low(w_up) * raw_up, axis=1)
        grad_gate = raw_gate * gain_two
        grad_up = raw_up * gain_two

        grad_attn = (BRANCH_SCALE * grad_middle).astype(BF16)
        grad_mixed = mm(grad_attn, out_w, ((1,), (1,))).astype(BF16)
        grad_mixed = exchange(grad_mixed.reshape(rows, n, block).transpose(1, 0, 2))
        grad_mixed = grad_mixed.reshape(n, rows, slots, HD)
        grad_attn_cols = exchange(grad_attn.reshape(rows, n, depth).transpose(1, 0, 2))
        grad_out = to_rows(
            mm(mixed_all[:, :width], grad_attn_cols.reshape(all_rows, depth), ((0,), (0,)))
        ).reshape(depth, width)
        grad_values = jnp.einsum("rhqk,rqhd->rkhd", probs_low, grad_mixed, preferred_element_type=F32)
        grad_probs = jnp.einsum("rqhd,rkhd->rhqk", grad_mixed, values, preferred_element_type=F32)
        grad_scores = (
            probs * (grad_probs - jnp.sum(probs * grad_probs, axis=-1, keepdims=True))
        ).astype(BF16)
        grad_query = jnp.einsum("rhqk,rkhd->rqhd", grad_scores, keys, preferred_element_type=F32)
        grad_keys = jnp.einsum("rhqk,rqhd->rkhd", grad_scores, query, preferred_element_type=F32)
        grad_query = rotate(grad_query * HD**-0.5, cosine, -sine)
        grad_keys = rotate(grad_keys * HD**-0.5, cosine, -sine)
        grad_qkv = jnp.concatenate(
            [g.astype(BF16).reshape(all_rows, block) for g in (grad_query, grad_keys, grad_values)],
            axis=1,
        )
        grad_normed_one = scatter_shard(mm(grad_qkv, qkv_w, ((1,), (1,))).astype(BF16)).astype(F32)
        my_inputs = tokens.astype(F32)
        my_scale_one = lax.rsqrt(jnp.mean(my_inputs * my_inputs, axis=-1, keepdims=True) + EPSILON)
        my_normed_one = my_inputs * my_scale_one
        inner_mean = jnp.mean(grad_normed_one * my_normed_one, axis=-1, keepdims=True)
        input_grad = grad_middle + my_scale_one * (grad_normed_one - my_normed_one * inner_mean)
        grad_attn_w = to_rows(mm(normed_one, grad_qkv, ((0,), (0,))))
        raw_query, raw_key, raw_value = (
            grad_attn_w[:, :, k * block : (k + 1) * block].reshape(depth, n * block)[:, :width]
            for k in range(3)
        )
        grad_gain_one = jnp.sum(
            low(w_query) * raw_query + low(w_key) * raw_key + low(w_value) * raw_value, axis=1
        )
        return (
            out_tokens,
            input_grad,
            grad_gain_one,
            raw_query * gain_one,
            raw_key * gain_one,
            raw_value * gain_one,
            grad_out,
            grad_gain_two,
            grad_gate,
            grad_up,
            grad_down,
        )

    return local


def solution(mesh):
    tokens = P(("rep", "shard"), None)
    weight = P("shard", None)
    gain = P("shard")
    return jax.shard_map(
        build(mesh.shape["rep"], mesh.shape["shard"]),
        mesh=mesh,
        in_specs=(
            tokens,
            tokens,
            tokens,
            gain,
            weight,
            weight,
            weight,
            weight,
            gain,
            weight,
            weight,
            weight,
            tokens,
        ),
        out_specs=(
            tokens,
            tokens,
            gain,
            weight,
            weight,
            weight,
            weight,
            gain,
            weight,
            weight,
            weight,
        ),
        check_vma=False,
    )
```

```python
import functools
import math

import jax
import jax.numpy as jnp
from jax import lax
from jax.experimental import pallas as pl
from jax.experimental.pallas import tpu as pltpu
from jax.sharding import PartitionSpec as P

HD = 64
HALF = HD // 2
PIC = 64

EPSILON = 1e-05
BRANCH_SCALE = 1.4 / math.sqrt(40.0)
MASKED = -1e30
F32 = jnp.float32
BF16 = jnp.bfloat16


def mm(left, right, left_dim, right_dim):
    return lax.dot_general(
        left, right, (((left_dim,), (right_dim,)), ((), ())), preferred_element_type=F32
    )


def layout(lengths, starts, row_count):
    places = jnp.arange(row_count, dtype=jnp.int32)
    bounds = jnp.cumsum(lengths)
    firsts = bounds - lengths
    member = (places[:, None] >= firsts[None, :]) & (places[:, None] < bounds[None, :])
    doc_of = jnp.sum(
        jnp.where(member, jnp.arange(lengths.shape[0], dtype=jnp.int32)[None, :], 0), axis=1
    )
    starting = jnp.sum(jnp.where(member, firsts[None, :], 0), axis=1)
    inside = (places[None, :] >= starts[:, None]) & (places[None, :] < starts[:, None] + PIC)
    shared = jnp.any(inside[:, :, None] & inside[:, None, :], axis=0)
    causal = places[None, :] >= places[:, None]
    allowed = (doc_of[:, None] == doc_of[None, :]) & (causal | shared)
    return (places - starting, allowed)


def turn(values, cosine, sine):
    first, second = values[:HALF], values[HALF:]
    return jnp.concatenate([first * cosine - second * sine, second * cosine + first * sine], axis=0)


def probabilities(keys, query, bias):
    scores = mm(keys, query, 0, 0) * HD**-0.5 + bias
    expo = jnp.exp(scores - jnp.max(scores, axis=0, keepdims=True))
    return expo / jnp.sum(expo, axis=0, keepdims=True)


def attend_kernel(slots, qkv_ref, scale_ref, cos_ref, sin_ref, bias_ref, qkv_out_ref, mixed_ref):
    block = slots * HD
    scale = scale_ref[...]
    cosine, sine, bias = cos_ref[...], sin_ref[...], bias_ref[0]
    for head in range(slots):
        low, high = head * HD, (head + 1) * HD
        query = turn(qkv_ref[low:high, :] * scale, cosine, sine).astype(BF16)
        keys = turn(qkv_ref[block + low : block + high, :] * scale, cosine, sine).astype(BF16)
        values = (qkv_ref[2 * block + low : 2 * block + high, :] * scale).astype(BF16)
        qkv_out_ref[low:high, :] = query
        qkv_out_ref[block + low : block + high, :] = keys
        qkv_out_ref[2 * block + low : 2 * block + high, :] = values
        probs = probabilities(keys, query, bias).astype(BF16)
        mixed_ref[low:high, :] = mm(values, probs, 1, 0).astype(BF16)


def attend_back_kernel(slots, qkv_ref, grad_ref, scale_ref, cos_ref, sin_ref, bias_ref, out_ref):
    block = slots * HD
    scale = scale_ref[...]
    cosine, sine, bias = cos_ref[...], sin_ref[...], bias_ref[0]
    back = scale * HD**-0.5
    for head in range(slots):
        low, high = head * HD, (head + 1) * HD
        query = qkv_ref[low:high, :]
        keys = qkv_ref[block + low : block + high, :]
        values = qkv_ref[2 * block + low : 2 * block + high, :]
        grad = grad_ref[low:high, :]
        probs = probabilities(keys, query, bias)
        grad_values = mm(grad, probs.astype(BF16), 1, 1)
        grad_probs = mm(values, grad, 0, 0)
        inner = jnp.sum(probs * grad_probs, axis=0, keepdims=True)
        grad_scores = (probs * (grad_probs - inner)).astype(BF16)
        grad_query = turn(mm(keys, grad_scores, 1, 0) * back, cosine, -sine)
        grad_keys = turn(mm(query, grad_scores, 1, 1) * back, cosine, -sine)
        out_ref[low:high, :] = grad_query.astype(BF16)
        out_ref[block + low : block + high, :] = grad_keys.astype(BF16)
        out_ref[2 * block + low : 2 * block + high, :] = (grad_values * scale).astype(BF16)


def columns(height, rows):
    return pl.BlockSpec((height, rows), lambda r: (0, r))


def attention_specs(rows):
    return [
        columns(1, rows),
        columns(HALF, rows),
        columns(HALF, rows),
        pl.BlockSpec((1, rows, rows), lambda r: (r, 0, 0)),
    ]


def attend(slots, n, rows, qkv, scale, cosine, sine, bias):
    block = slots * HD
    tokens = n * rows
    flops = 4 * n * slots * rows * rows * HD
    return pl.pallas_call(
        functools.partial(attend_kernel, slots),
        grid=(n,),
        in_specs=[columns(3 * block, rows)] + attention_specs(rows),
        out_specs=[columns(3 * block, rows), columns(block, rows)],
        out_shape=[
            jax.ShapeDtypeStruct((3 * block, tokens), BF16),
            jax.ShapeDtypeStruct((block, tokens), BF16),
        ],
        cost_estimate=pl.CostEstimate(
            flops=flops, bytes_accessed=20 * block * tokens, transcendentals=n * slots * rows * rows
        ),
        name="attend",
    )(qkv, scale, cosine, sine, bias)


def attend_back(slots, n, rows, qkv, grad, scale, cosine, sine, bias):
    block = slots * HD
    tokens = n * rows
    flops = 10 * n * slots * rows * rows * HD
    return pl.pallas_call(
        functools.partial(attend_back_kernel, slots),
        grid=(n,),
        in_specs=[columns(3 * block, rows), columns(block, rows)] + attention_specs(rows),
        out_specs=columns(3 * block, rows),
        out_shape=jax.ShapeDtypeStruct((3 * block, tokens), BF16),
        cost_estimate=pl.CostEstimate(
            flops=flops, bytes_accessed=14 * block * tokens, transcendentals=n * slots * rows * rows
        ),
        name="attend_back",
    )(qkv, grad, scale, cosine, sine, bias)


def build(rep, n):
    cycle = list(range(0, n, 2)) + list(range(n - 1, 0, -2)) if n % 2 == 0 else list(range(n))
    place = [cycle.index(device) for device in range(n)]
    to_right = [(cycle[i], cycle[(i + 1) % n]) for i in range(n)]
    to_left = [(b, a) for a, b in to_right]
    steps_right = n // 2
    steps_left = n - 1 - steps_right
    outer = rep // 2
    core_pairs = [(i, i ^ 1) for i in range(rep)]
    chip_pairs = [(i, (i + 2) % rep) for i in range(rep)]

    def right(x):
        return lax.ppermute(x, "shard", to_right)

    def left(x):
        return lax.ppermute(x, "shard", to_left)

    def core_swap(x):
        return lax.ppermute(x, "rep", core_pairs)

    def chip_swap(x):
        return lax.ppermute(x, "rep", chip_pairs)

    def ring_device(offset):
        at = jnp.asarray(place, jnp.int32)[lax.axis_index("shard")]
        return jnp.asarray(cycle, jnp.int32)[(at + offset) % n]

    def ring_gather(piece):
        pieces = [(ring_device(0), piece)]
        going_right = going_left = piece
        for step in range(1, steps_right + 1):
            going_right = right(going_right)
            pieces.append((ring_device(-step), going_right))
            if step <= steps_left:
                going_left = left(going_left)
                pieces.append((ring_device(step), going_left))
        return pieces

    def gather_shard(piece):
        whole = jnp.zeros((n,) + piece.shape, piece.dtype)
        for device, part in ring_gather(piece):
            whole = lax.dynamic_update_index_in_dim(whole, part, device, 0)
        return whole

    def scatter_shard(parts):
        def term(offset):
            return lax.dynamic_index_in_dim(parts, ring_device(offset), 0, keepdims=False).astype(F32)

        going_right = term(steps_right).astype(BF16)
        going_left = term(-steps_left).astype(BF16)
        for step in range(1, steps_right + 1):
            going_right = right(going_right)
            if step < steps_right:
                going_right = (going_right.astype(F32) + term(steps_right - step)).astype(BF16)
            if step <= steps_left:
                going_left = left(going_left)
                if step < steps_left:
                    going_left = (going_left.astype(F32) + term(step - steps_left)).astype(BF16)
        return going_right.astype(F32) + going_left.astype(F32) + term(0)

    def exchange(blocks):
        return lax.all_to_all(blocks, "shard", split_axis=0, concat_axis=0, tiled=True)

    def pick(array, index, axis):
        return lax.dynamic_index_in_dim(array, index, axis, keepdims=False)

    def add(a, b):
        return (a.astype(F32) + b.astype(F32)).astype(BF16)

    def gather_rep(piece):
        mine = lax.axis_index("rep")
        other_chip = chip_swap(piece)
        other_core = core_swap(piece)
        last = core_swap(other_chip)
        whole = jnp.zeros((rep,) + piece.shape, piece.dtype)
        far = (mine + 2) % rep
        for index, part in ((mine, piece), (far, other_chip), (mine ^ 1, other_core), (far ^ 1, last)):
            whole = lax.dynamic_update_index_in_dim(whole, part, index, 0)
        return whole

    def scatter_rep(blocks):
        mine = lax.axis_index("rep")
        chip, core = mine // 2, mine % 2
        blocks = blocks.reshape((blocks.shape[0], outer, 2) + blocks.shape[2:])
        half = add(pick(blocks, core, 2), core_swap(pick(blocks, 1 - core, 2)))
        return add(pick(half, chip, 1), chip_swap(pick(half, 1 - chip, 1)))

    def local(
        tokens,
        doc_lengths,
        pic_starts,
        attn_gain,
        w_query,
        w_key,
        w_value,
        w_out,
        ffn_gain,
        w_gate,
        w_up,
        w_down,
        cotangent,
    ):
        rows, width = tokens.shape
        heads = width // HD
        base = heads // n
        slots = -(-heads // n)
        block = slots * HD
        main = base * HD
        mains = n * main
        depth = w_query.shape[0]
        part = depth // rep
        ff = w_gate.shape[1]
        cols = ff // n
        all_rows = n * rows
        me = lax.axis_index("shard")
        mine = lax.axis_index("rep")
        gain_one = attn_gain.astype(BF16).astype(F32)[:, None]
        gain_two = ffn_gain.astype(BF16).astype(F32)[:, None]
        docs = doc_lengths.shape[1]
        pics = pic_starts.shape[1]

        def quarter(array):
            return lax.dynamic_slice_in_dim(array, mine * part, part, 0)

        def scaled(weight, gain):
            return (quarter(weight).astype(BF16).astype(F32) * quarter(gain)).astype(BF16)

        def by_heads(array, axis):
            if slots == base:
                return jnp.moveaxis(
                    array.reshape(array.shape[:axis] + (n, main) + array.shape[axis + 1 :]), axis, 0
                )
            first = lax.slice_in_dim(array, 0, mains, axis=axis)
            rest = lax.slice_in_dim(array, mains, width, axis=axis)
            pad = [(0, 0)] * array.ndim
            pad[axis] = (0, n * HD - (width - mains))
            rest = jnp.pad(rest, pad)
            split = [
                jnp.moveaxis(a.reshape(a.shape[:axis] + (n, size) + a.shape[axis + 1 :]), axis, 0)
                for a, size in ((first, main), (rest, HD))
            ]
            return jnp.concatenate(split, axis=axis + 1)

        def from_heads(array):
            first = array[:, :, :main].transpose(1, 0, 2).reshape(array.shape[1], mains)
            if slots == base:
                return first
            over = (width - mains) // HD
            rest = array[:over, :, main:].transpose(1, 0, 2).reshape(array.shape[1], width - mains)
            return jnp.concatenate([first, rest], axis=1)

        info = jnp.concatenate([doc_lengths[0], pic_starts[0]]).astype(BF16)
        info = jnp.zeros((n, 8, 3 * block), BF16).at[:, 0, : docs + pics].set(info)
        qkv_part = jnp.concatenate(
            [by_heads(scaled(w, gain_one), 1) for w in (w_query, w_key, w_value)], axis=2
        )
        qkv_part = exchange(jnp.concatenate([qkv_part, info], axis=1))
        info = qkv_part[:, part, : docs + pics].astype(jnp.int32)
        qkv_w = gather_rep(qkv_part[:, :part]).transpose(1, 0, 2, 3).reshape(width, 3 * block)
        out_part = gather_shard(quarter(w_out).astype(BF16))
        out_w = gather_rep(out_part).transpose(1, 0, 2, 3).reshape(width, width)
        ffn_part = jnp.concatenate(
            [scaled(w, gain_two).reshape(part, n, cols).transpose(1, 0, 2) for w in (w_gate, w_up)],
            axis=1,
        )
        ffn_w = gather_rep(exchange(ffn_part)).reshape(rep, n, 2, part, cols)
        ffn_w = ffn_w.transpose(2, 1, 0, 3, 4).reshape(2, width, cols)
        gate_w, up_w = ffn_w[0], ffn_w[1]
        down_w = w_down.astype(BF16)

        inputs = gather_shard(tokens).reshape(all_rows, width)
        offsets, allowed = jax.vmap(lambda a, b: layout(a, b, rows))(info[:, :docs], info[:, docs:])
        bias = jnp.where(allowed, 0.0, MASKED).astype(F32)
        freq_table = jnp.exp(jnp.arange(HALF, dtype=F32) * (-2.0 * math.log(10000.0) / HD))
        turned = freq_table[:, None] * offsets.reshape(1, all_rows).astype(F32)
        cosine, sine = jnp.cos(turned), jnp.sin(turned)
        squares = jnp.mean(jnp.square(inputs.astype(F32)), axis=-1)
        scale_one = lax.rsqrt(squares + EPSILON)[None, :]
        qkv = mm(qkv_w, inputs, 0, 1)
        qkv, mixed = attend(slots, n, rows, qkv, scale_one, cosine, sine, bias)
        mixed_all = jnp.zeros((n * block, all_rows), BF16)
        for device, piece in ring_gather(mixed):
            mixed_all = lax.dynamic_update_slice_in_dim(mixed_all, piece[:main], device * main, 0)
            if slots > base:
                mixed_all = lax.dynamic_update_slice_in_dim(
                    mixed_all, piece[main:], mains + device * HD, 0
                )
        mixed_all = mixed_all[:width]
        middle = inputs.astype(F32) + BRANCH_SCALE * mm(mixed_all, out_w, 0, 0)

        scale_two = lax.rsqrt(jnp.mean(middle * middle, axis=-1, keepdims=True) + EPSILON)
        middle_low = middle.astype(BF16)
        gate_act = mm(middle_low, gate_w, 1, 0) * scale_two
        up_act = mm(middle_low, up_w, 1, 0) * scale_two
        sigmoid_gate = jax.nn.sigmoid(gate_act)
        silu_gate = gate_act * sigmoid_gate
        inner = (silu_gate * up_act).astype(BF16)
        grad_result = cotangent.astype(F32)
        grad_branch = gather_shard((BRANCH_SCALE * grad_result).astype(BF16)).reshape(all_rows, width)
        grad_inner = mm(grad_branch, down_w, 1, 1)
        grad_gate_act = (
            grad_inner
            * up_act
            * sigmoid_gate
            * (1.0 + gate_act * (1.0 - sigmoid_gate))
            * scale_two
        ).astype(BF16)
        grad_up_act = (grad_inner * silu_gate * scale_two).astype(BF16)
        partial = mm(grad_gate_act, gate_w, 1, 1) + mm(grad_up_act, up_w, 1, 1)
        back_two = scatter_shard(partial.astype(BF16).reshape(n, rows, width))
        my_middle = lax.dynamic_slice_in_dim(middle, me * rows, rows, 0)
        my_normed_two = my_middle * lax.dynamic_slice_in_dim(scale_two, me * rows, rows, 0)
        inner_mean = jnp.mean(back_two * my_normed_two, axis=-1, keepdims=True)
        grad_middle = grad_result + back_two - my_normed_two * inner_mean

        grad_attn = (BRANCH_SCALE * grad_middle).astype(BF16)
        grad_mixed = exchange(by_heads(mm(out_w, grad_attn, 1, 1).astype(BF16), 0))
        grad_mixed = grad_mixed.transpose(1, 0, 2).reshape(block, all_rows)
        grad_attn_cols = exchange(grad_attn.T.reshape(n, depth, rows))
        grad_attn_cols = grad_attn_cols.transpose(1, 0, 2).reshape(depth, all_rows)
        grad_qkv = attend_back(
            slots, n, rows, qkv, grad_mixed, scale_one, cosine, sine, bias
        )
        partial = mm(grad_qkv, qkv_w, 0, 1)
        back_one = scatter_shard(partial.astype(BF16).reshape(n, rows, width))
        my_inputs = tokens.astype(F32)
        my_scale_one = lax.rsqrt(jnp.mean(my_inputs * my_inputs, axis=-1, keepdims=True) + EPSILON)
        my_normed_one = my_inputs * my_scale_one
        inner_mean = jnp.mean(back_one * my_normed_one, axis=-1, keepdims=True)
        input_grad = grad_middle + back_one - my_normed_one * inner_mean

        branch = scatter_shard(mm(inner, down_w, 1, 0).astype(BF16).reshape(n, rows, width))
        out_tokens = (my_middle + BRANCH_SCALE * branch).astype(BF16)

        def rep_rows(grad):
            return grad.astype(BF16).reshape(n, rep, part, grad.shape[1])

        def low(weight):
            return weight.astype(BF16).astype(F32)

        grad_down = mm(inner, grad_branch, 0, 0).astype(BF16).reshape(1, rep, -1, width)
        grad_down = gather_rep(scatter_rep(grad_down)[0]).reshape(-1, width).astype(F32)

        grad_ffn = [rep_rows(mm(middle_low, g, 0, 0)) for g in (grad_gate_act, grad_up_act)]
        grad_ffn = exchange(scatter_rep(jnp.concatenate(grad_ffn, axis=2).reshape(n, rep, -1, cols)))
        grad_ffn = grad_ffn.reshape(n, 2, part, cols).transpose(1, 2, 0, 3).reshape(2, part, ff)
        grad_ffn = gather_rep(grad_ffn).transpose(1, 0, 2, 3).reshape(2, depth, ff).astype(F32)
        grad_gain_two = jnp.sum(low(w_gate) * grad_ffn[0] + low(w_up) * grad_ffn[1], axis=1)

        grad_out = exchange(scatter_rep(rep_rows(mm(mixed_all, grad_attn_cols, 1, 1))))
        grad_out = grad_out.transpose(1, 0, 2).reshape(part, width)
        grad_out = gather_rep(grad_out).reshape(depth, width).astype(F32)

        grad_w = exchange(scatter_rep(rep_rows(mm(inputs, grad_qkv, 0, 1))))
        grad_w = jnp.stack([from_heads(grad_w[:, :, k * block : (k + 1) * block]) for k in range(3)])
        grad_w = gather_rep(grad_w).transpose(1, 0, 2, 3).reshape(3, depth, width).astype(F32)
        grad_gain_one = jnp.sum(
            low(w_query) * grad_w[0] + low(w_key) * grad_w[1] + low(w_value) * grad_w[2], axis=1
        )
        return (
            out_tokens,
            input_grad,
            grad_gain_one,
            grad_w[0] * gain_one,
            grad_w[1] * gain_one,
            grad_w[2] * gain_one,
            grad_out,
            grad_gain_two,
            grad_ffn[0] * gain_two,
            grad_ffn[1] * gain_two,
            grad_down,
        )

    return local


def solution(mesh):
    tokens = P(("rep", "shard"), None)
    weight = P("shard", None)
    gain = P("shard")
    return jax.shard_map(
        build(mesh.shape["rep"], mesh.shape["shard"]),
        mesh=mesh,
        in_specs=(
            tokens,
            tokens,
            tokens,
            gain,
            weight,
            weight,
            weight,
            weight,
            gain,
            weight,
            weight,
            weight,
            tokens,
        ),
        out_specs=(
            tokens,
            tokens,
            gain,
            weight,
            weight,
            weight,
            weight,
            gain,
            weight,
            weight,
            weight,
        ),
        check_vma=False,
    )
```

```python
import functools
import math

import jax
import jax.numpy as jnp
from jax import lax
from jax.experimental import pallas as pl
from jax.experimental.layout import Layout, with_layout_constraint
from jax.experimental.pallas import tpu as pltpu
from jax.sharding import PartitionSpec as P

HD = 64
HALF = HD // 2
PIC = 64

EPSILON = 1e-05
BRANCH_SCALE = 1.4 / math.sqrt(40.0)
MASKED = -1e30
F32 = jnp.float32
BF16 = jnp.bfloat16


def mm(left, right, left_dim, right_dim):
    return lax.dot_general(
        left, right, (((left_dim,), (right_dim,)), ((), ())), preferred_element_type=F32
    )


def layout(lengths, starts, row_count):
    places = jnp.arange(row_count, dtype=jnp.int32)
    bounds = jnp.cumsum(lengths)
    firsts = bounds - lengths
    member = (places[:, None] >= firsts[None, :]) & (places[:, None] < bounds[None, :])
    doc_of = jnp.sum(
        jnp.where(member, jnp.arange(lengths.shape[0], dtype=jnp.int32)[None, :], 0), axis=1
    )
    starting = jnp.sum(jnp.where(member, firsts[None, :], 0), axis=1)
    inside = (places[None, :] >= starts[:, None]) & (places[None, :] < starts[:, None] + PIC)
    shared = jnp.any(inside[:, :, None] & inside[:, None, :], axis=0)
    causal = places[None, :] >= places[:, None]
    allowed = (doc_of[:, None] == doc_of[None, :]) & (causal | shared)
    return (places - starting, allowed)


def turn(values, cosine, sine):
    first, second = values[:HALF], values[HALF:]
    return jnp.concatenate([first * cosine - second * sine, second * cosine + first * sine], axis=0)


def probabilities(keys, query, bias):
    scores = mm(keys, query, 0, 0) * HD**-0.5 + bias
    expo = jnp.exp(scores - jnp.max(scores, axis=0, keepdims=True))
    return expo / jnp.sum(expo, axis=0, keepdims=True)


def feature_rows(base, slots, kind, head):
    if head < base:
        return (kind * base + head) * HD
    return (3 * base + kind * (slots - base) + head - base) * HD


def attend_kernel(base, slots, qkv_ref, scale_ref, cos_ref, sin_ref, bias_ref, qkv_out_ref, mixed_ref):
    scale = scale_ref[...]
    cosine, sine, bias = cos_ref[...], sin_ref[...], bias_ref[0]
    for head in range(slots):
        at = [pl.ds(feature_rows(base, slots, kind, head), HD) for kind in range(3)]
        query = turn(qkv_ref[at[0], :] * scale, cosine, sine).astype(BF16)
        keys = turn(qkv_ref[at[1], :] * scale, cosine, sine).astype(BF16)
        values = (qkv_ref[at[2], :] * scale).astype(BF16)
        qkv_out_ref[at[0], :] = query
        qkv_out_ref[at[1], :] = keys
        qkv_out_ref[at[2], :] = values
        probs = probabilities(keys, query, bias).astype(BF16)
        mixed_ref[pl.ds(head * HD, HD), :] = mm(values, probs, 1, 0).astype(BF16)


def attend_back_kernel(base, slots, qkv_ref, grad_ref, scale_ref, cos_ref, sin_ref, bias_ref, out_ref):
    scale = scale_ref[...]
    cosine, sine, bias = cos_ref[...], sin_ref[...], bias_ref[0]
    back = scale * HD**-0.5
    for head in range(slots):
        at = [pl.ds(feature_rows(base, slots, kind, head), HD) for kind in range(3)]
        query = qkv_ref[at[0], :]
        keys = qkv_ref[at[1], :]
        values = qkv_ref[at[2], :]
        grad = grad_ref[pl.ds(head * HD, HD), :]
        probs = probabilities(keys, query, bias)
        grad_values = mm(grad, probs.astype(BF16), 1, 1)
        grad_probs = mm(values, grad, 0, 0)
        inner = jnp.sum(probs * grad_probs, axis=0, keepdims=True)
        grad_scores = (probs * (grad_probs - inner)).astype(BF16)
        grad_query = turn(mm(keys, grad_scores, 1, 0) * back, cosine, -sine)
        grad_keys = turn(mm(query, grad_scores, 1, 1) * back, cosine, -sine)
        out_ref[at[0], :] = grad_query.astype(BF16)
        out_ref[at[1], :] = grad_keys.astype(BF16)
        out_ref[at[2], :] = (grad_values * scale).astype(BF16)


def columns(height, rows):
    return pl.BlockSpec((height, rows), lambda r: (0, r))


def attention_specs(rows):
    return [
        columns(1, rows),
        columns(HALF, rows),
        columns(HALF, rows),
        pl.BlockSpec((1, rows, rows), lambda r: (r, 0, 0)),
    ]


def attend(base, slots, n, rows, qkv, scale, cosine, sine, bias):
    block = slots * HD
    tokens = n * rows
    flops = 4 * n * slots * rows * rows * HD
    return pl.pallas_call(
        functools.partial(attend_kernel, base, slots),
        grid=(n,),
        in_specs=[columns(3 * block, rows)] + attention_specs(rows),
        out_specs=[columns(3 * block, rows), columns(block, rows)],
        out_shape=[
            jax.ShapeDtypeStruct((3 * block, tokens), BF16),
            jax.ShapeDtypeStruct((block, tokens), BF16),
        ],
        cost_estimate=pl.CostEstimate(
            flops=flops, bytes_accessed=20 * block * tokens, transcendentals=n * slots * rows * rows
        ),
        compiler_params=pltpu.CompilerParams(vmem_limit_bytes=12 * 2**20),
        name="attend",
    )(qkv, scale, cosine, sine, bias)


def attend_back(base, slots, n, rows, qkv, grad, scale, cosine, sine, bias):
    block = slots * HD
    tokens = n * rows
    flops = 10 * n * slots * rows * rows * HD
    return pl.pallas_call(
        functools.partial(attend_back_kernel, base, slots),
        grid=(n,),
        in_specs=[columns(3 * block, rows), columns(block, rows)] + attention_specs(rows),
        out_specs=columns(3 * block, rows),
        out_shape=jax.ShapeDtypeStruct((3 * block, tokens), BF16),
        cost_estimate=pl.CostEstimate(
            flops=flops, bytes_accessed=14 * block * tokens, transcendentals=n * slots * rows * rows
        ),
        compiler_params=pltpu.CompilerParams(vmem_limit_bytes=16 * 2**20),
        name="attend_back",
    )(qkv, grad, scale, cosine, sine, bias)


def row_major(array):
    return with_layout_constraint(array, Layout(tuple(range(array.ndim))))


def empty(shape, dtype):
    return pl.pallas_call(
        lambda out_ref: None,
        out_specs=pl.BlockSpec(memory_space=pl.ANY),
        out_shape=jax.ShapeDtypeStruct(shape, dtype),
        compiler_params=pltpu.CompilerParams(vmem_limit_bytes=1 * 2**20),
        name="empty",
    )()


def low(weight):
    return weight.astype(BF16).astype(F32)


def prepare_kernel(n, base, slots, heads, own_ref, query_ref, key_ref, value_ref, gain_ref, info_ref, out_ref):
    part = query_ref.shape[1]
    main = base * HD
    for kind, ref in enumerate((query_ref, key_ref, value_ref)):
        weight = (low(ref[0]) * gain_ref[0]).astype(BF16)
        for j in range(n):
            out_ref[j, :part, kind * main : (kind + 1) * main] = weight[:, j * main : (j + 1) * main]
            if slots > base:
                first = 3 * main + kind * HD
                head = n * base + j
                if head < heads:
                    extra = weight[:, head * HD : (head + 1) * HD]
                else:
                    extra = jnp.zeros((part, HD), BF16)
                out_ref[j, :part, first : first + HD] = extra
    for j in range(n):
        out_ref[j, part:, :] = info_ref[...]


def prepare_ffn_kernel(n, own_ref, gate_ref, up_ref, gain_ref, out_ref):
    part, cols = gate_ref.shape[1], out_ref.shape[2]
    for kind, ref in enumerate((gate_ref, up_ref)):
        weight = (low(ref[0]) * gain_ref[0]).astype(BF16)
        for j in range(n):
            out_ref[j, kind * part : (kind + 1) * part, :] = weight[:, j * cols : (j + 1) * cols]


def own_part(part, width):
    return pl.BlockSpec((1, part, width), lambda i, own: (own[0], 0, 0))


def prepare(kernel, own, weights, gain, more, out_shape, name):
    part = weights[0].shape[1]
    return pl.pallas_call(
        kernel,
        grid_spec=pltpu.PrefetchScalarGridSpec(
            num_scalar_prefetch=1,
            grid=(1,),
            in_specs=[own_part(part, w.shape[2]) for w in weights]
            + [own_part(part, 1)]
            + [pl.BlockSpec(m.shape, lambda i, own: (0, 0)) for m in more],
            out_specs=pl.BlockSpec(out_shape, lambda i, own: (0, 0, 0)),
        ),
        out_shape=jax.ShapeDtypeStruct(out_shape, BF16),
        name=name,
    )(own, *weights, gain, *more)


def finish_kernel(count, gained, at_ref, piece_ref, *refs):
    weights = refs[:gained]
    outs = refs[-(count + (gained > 0)) :]
    total = 0.0
    for k in range(count):
        raw = piece_ref[k].astype(F32)
        if k < gained:
            total = total + jnp.sum(low(weights[k][0]) * raw, axis=1, keepdims=True)
            raw = raw * refs[gained][0]
        outs[k][0] = raw
    if gained:
        first = pl.program_id(0) == 0
        outs[count][0] = jnp.where(first, 0.0, outs[count][0]) + total


def finish(piece, at, rep, weights, gain, previous):
    count, part, width = piece.shape
    gained = len(weights)
    chunk = max(c for c in range(128, 1153, 128) if width % c == 0)

    def placed(size, moving):
        return pl.BlockSpec((1, part, size), lambda i, at: (at[0], 0, i if moving else 0))

    in_specs = [pl.BlockSpec((count, part, chunk), lambda i, at: (0, 0, i))]
    operands = [piece]
    out_specs = [placed(chunk, True)] * count
    out_shape = [jax.ShapeDtypeStruct((rep, part, width), F32)] * count
    if gained:
        in_specs += [placed(chunk, True)] * gained + [placed(1, False)]
        operands += list(weights) + [gain]
        out_specs.append(placed(1, False))
        out_shape.append(jax.ShapeDtypeStruct((rep, part, 1), F32))
    aliases = {}
    if previous is not None:
        aliases = {1 + len(operands) + k: k for k in range(len(out_shape))}
        operands += list(previous)
        in_specs += [pl.BlockSpec(memory_space=pl.ANY)] * len(out_shape)
    return pl.pallas_call(
        functools.partial(finish_kernel, count, gained),
        grid_spec=pltpu.PrefetchScalarGridSpec(
            num_scalar_prefetch=1, grid=(width // chunk,), in_specs=in_specs, out_specs=out_specs
        ),
        out_shape=out_shape,
        input_output_aliases=aliases,
        cost_estimate=pl.CostEstimate(
            flops=4 * count * part * width,
            bytes_accessed=(6 * count + 4 * gained) * part * width,
            transcendentals=0,
        ),
        name="finish",
    )(at, *operands)


def build(rep, n):
    cycle = list(range(0, n, 2)) + list(range(n - 1, 0, -2)) if n % 2 == 0 else list(range(n))
    to_right = [(cycle[i], cycle[(i + 1) % n]) for i in range(n)]
    to_left = [(b, a) for a, b in to_right]
    steps_right = n // 2
    steps_left = n - 1 - steps_right
    outer = rep // 2
    core_pairs = [(i, i ^ 1) for i in range(rep)]
    chip_pairs = [(i, (i + 2) % rep) for i in range(rep)]

    def right(x):
        return lax.ppermute(x, "shard", to_right)

    def left(x):
        return lax.ppermute(x, "shard", to_left)

    def core_swap(x):
        return lax.ppermute(x, "rep", core_pairs)

    def chip_swap(x):
        return lax.ppermute(x, "rep", chip_pairs)

    def ring_device(offset):
        device = lax.axis_index("shard")
        if n % 2:
            return (device + offset + n) % n
        place = jnp.where(device % 2 == 0, device // 2, n - 1 - device // 2)
        place = (place + offset + n) % n
        return jnp.where(place < n // 2, 2 * place, 2 * (n - 1 - place) + 1)

    def ring_gather(piece):
        pieces = [(ring_device(0), piece)]
        going_right = going_left = piece
        for step in range(1, steps_right + 1):
            going_right = right(going_right)
            pieces.append((ring_device(-step), going_right))
            if step <= steps_left:
                going_left = left(going_left)
                pieces.append((ring_device(step), going_left))
        return pieces

    def gather_shard(piece):
        pieces = ring_gather(piece)
        whole = empty((n,) + piece.shape, piece.dtype)
        for device, part in pieces:
            whole = lax.dynamic_update_index_in_dim(whole, part, device, 0)
        return whole.reshape((-1,) + piece.shape[1:]), pieces[-1][1]

    def scatter_shard(parts):
        def term(offset):
            return lax.dynamic_index_in_dim(parts, ring_device(offset), 0, keepdims=False).astype(F32)

        going_right = term(steps_right).astype(BF16)
        going_left = term(-steps_left).astype(BF16)
        for step in range(1, steps_right + 1):
            going_right = right(going_right)
            if step < steps_right:
                going_right = (going_right.astype(F32) + term(steps_right - step)).astype(BF16)
            if step <= steps_left:
                going_left = left(going_left)
                if step < steps_left:
                    going_left = (going_left.astype(F32) + term(step - steps_left)).astype(BF16)
        return going_right.astype(F32) + going_left.astype(F32) + term(0)

    def exchange(blocks):
        return lax.all_to_all(blocks, "shard", split_axis=0, concat_axis=0, tiled=True)

    def pick(array, index, axis):
        return lax.dynamic_index_in_dim(array, index, axis, keepdims=False)

    def add(a, b):
        return (a.astype(F32) + b.astype(F32)).astype(BF16)

    def after(value, *others):
        return lax.optimization_barrier((value, others))[0]

    def rep_pieces(piece):
        mine = lax.axis_index("rep")
        far = (mine + 2) % rep
        other_chip = chip_swap(piece)
        other_core = core_swap(piece)
        last = core_swap(other_chip)
        return [(mine, piece), (mine ^ 1, other_core), (far, other_chip), (far ^ 1, last)]

    def gather_rep(piece, axis):
        whole = empty(piece.shape[:axis] + (rep,) + piece.shape[axis:], piece.dtype)
        for index, part in rep_pieces(piece):
            whole = lax.dynamic_update_index_in_dim(whole, part, index, axis)
        return whole

    def scatter_rep(blocks):
        mine = lax.axis_index("rep")
        chip, core = mine // 2, mine % 2
        blocks = blocks.reshape((blocks.shape[0], outer, 2) + blocks.shape[2:])
        half = add(pick(blocks, core, 2), core_swap(pick(blocks, 1 - core, 2)))
        return add(pick(half, chip, 1), chip_swap(pick(half, 1 - chip, 1)))

    def local(
        tokens,
        doc_lengths,
        pic_starts,
        attn_gain,
        w_query,
        w_key,
        w_value,
        w_out,
        ffn_gain,
        w_gate,
        w_up,
        w_down,
        cotangent,
    ):
        rows, width = tokens.shape
        heads = width // HD
        base = heads // n
        slots = -(-heads // n)
        block = slots * HD
        main = base * HD
        mains = n * main
        over = heads - n * base
        depth = w_query.shape[0]
        part = depth // rep
        ff = w_gate.shape[1]
        cols = ff // n
        all_rows = n * rows
        me = lax.axis_index("shard")
        mine = lax.axis_index("rep")
        own = mine.reshape(1)
        docs = doc_lengths.shape[1]
        pics = pic_starts.shape[1]

        def by_rep(array):
            return array.reshape(rep, -1, array.shape[1])

        gain_one = by_rep(low(attn_gain)[:, None])
        gain_two = by_rep(low(ffn_gain)[:, None])

        def by_heads(array):
            first = array[:mains].reshape(n, main, -1)
            if slots == base:
                return first
            rest = jnp.pad(array[mains:], ((0, n * HD - (width - mains)), (0, 0)))
            return jnp.concatenate([first, rest.reshape(n, HD, -1)], axis=1)

        def from_heads(array, kind):
            first = array[:, :, kind * main : (kind + 1) * main].transpose(1, 0, 2)
            first = first.reshape(array.shape[1], mains)
            if slots == base:
                return first
            start = 3 * main + kind * HD
            rest = array[:over, :, start : start + HD].transpose(1, 0, 2)
            return jnp.concatenate([first, rest.reshape(array.shape[1], width - mains)], axis=1)

        inputs, last_input = gather_shard(tokens)
        info = jnp.concatenate([doc_lengths[0], pic_starts[0]]).astype(BF16)
        info = jnp.zeros((8, 3 * block), BF16).at[0, : docs + pics].set(info)
        qkv_part = prepare(
            functools.partial(prepare_kernel, n, base, slots, heads),
            own,
            [by_rep(w) for w in (w_query, w_key, w_value)],
            gain_one,
            [info],
            (n, part + 8, 3 * block),
            "prepare_qkv",
        )
        qkv_part = exchange(qkv_part)
        info = qkv_part[:, part, : docs + pics].astype(jnp.int32)
        qkv_w = gather_rep(qkv_part[:, :part], 1).reshape(width, 3 * block)
        out_part = after(pick(by_rep(w_out), mine, 0), last_input).astype(BF16)
        out_w = lax.all_gather(out_part, ("shard", "rep"), axis=0, tiled=True)
        ffn_part = prepare(
            functools.partial(prepare_ffn_kernel, n),
            own,
            [by_rep(w) for w in (w_gate, w_up)],
            gain_two,
            [],
            (n, 2 * part, cols),
            "prepare_ffn",
        )
        ffn_part = exchange(after(ffn_part, qkv_part, last_input))
        down_w = w_down.astype(BF16)
        grad_result = cotangent.astype(F32)

        offsets, allowed = jax.vmap(lambda a, b: layout(a, b, rows))(info[:, :docs], info[:, docs:])
        bias = jnp.where(allowed, 0.0, MASKED).astype(F32)
        freq_table = jnp.exp(jnp.arange(HALF, dtype=F32) * (-2.0 * math.log(10000.0) / HD))
        turned = freq_table[:, None] * offsets.reshape(1, all_rows).astype(F32)
        cosine, sine = jnp.cos(turned), jnp.sin(turned)
        squares = jnp.mean(jnp.square(inputs.astype(F32)), axis=-1)
        scale_one = lax.rsqrt(squares + EPSILON)[None, :]
        qkv = mm(qkv_w, inputs, 0, 1)
        qkv, mixed = attend(base, slots, n, rows, qkv, scale_one, cosine, sine, bias)
        ffn_part = after(ffn_part, mixed)
        ffn_w = gather_rep(ffn_part.reshape(n, 2, part, cols).transpose(1, 0, 2, 3), 2)
        gate_w = ffn_w[0].reshape(width, cols)
        up_w = ffn_w[1].reshape(width, cols)
        mixed_all = empty((n * block, all_rows), BF16)
        mixed_pieces = ring_gather(mixed)
        for device, piece in mixed_pieces:
            mixed_all = lax.dynamic_update_slice_in_dim(mixed_all, piece[:main], device * main, 0)
            if slots > base:
                mixed_all = lax.dynamic_update_slice_in_dim(
                    mixed_all, piece[main:], mains + device * HD, 0
                )
        mixed_all = mixed_all[:width]
        middle = inputs.astype(F32) + BRANCH_SCALE * mm(mixed_all, out_w, 0, 0)

        grad_branch = after((BRANCH_SCALE * grad_result).astype(BF16), mixed_pieces[-1][1])
        grad_branch, _ = gather_shard(grad_branch)
        scale_two = lax.rsqrt(jnp.mean(middle * middle, axis=-1, keepdims=True) + EPSILON)
        middle_low = middle.astype(BF16)
        gate_act = mm(middle_low, gate_w, 1, 0) * scale_two
        up_act = mm(middle_low, up_w, 1, 0) * scale_two
        sigmoid_gate = jax.nn.sigmoid(gate_act)
        silu_gate = gate_act * sigmoid_gate
        inner = (silu_gate * up_act).astype(BF16)
        grad_inner = mm(grad_branch, down_w, 1, 1)
        grad_gate_act = (
            grad_inner
            * up_act
            * sigmoid_gate
            * (1.0 + gate_act * (1.0 - sigmoid_gate))
            * scale_two
        ).astype(BF16)
        grad_up_act = (grad_inner * silu_gate * scale_two).astype(BF16)
        partial = mm(grad_gate_act, gate_w, 1, 1) + mm(grad_up_act, up_w, 1, 1)
        partial = partial.astype(BF16).reshape(n, rows, width)
        back_two = scatter_shard(partial)
        my_middle = lax.dynamic_slice_in_dim(middle, me * rows, rows, 0)
        my_normed_two = my_middle * lax.dynamic_slice_in_dim(scale_two, me * rows, rows, 0)
        inner_mean = jnp.mean(back_two * my_normed_two, axis=-1, keepdims=True)
        grad_middle = grad_result + back_two - my_normed_two * inner_mean

        def rep_rows(grad):
            return row_major(grad.astype(BF16)).reshape(n, rep, part, grad.shape[1])

        def finish_all(piece, weights, gain):
            done = None
            for index, arrived in rep_pieces(piece):
                done = finish(
                    arrived, index.reshape(1), rep, [by_rep(w) for w in weights], gain, done
                )
            return [a.reshape(-1, a.shape[2]) for a in done]

        inner, grad_gate_act, grad_up_act, _ = lax.optimization_barrier(
            (inner, grad_gate_act, grad_up_act, partial)
        )
        grad_down = mm(inner, grad_branch, 0, 0).astype(BF16).reshape(1, rep, -1, width)
        (grad_down,) = finish_all(scatter_rep(grad_down), (), None)
        grad_ffn = [rep_rows(mm(middle_low, g, 0, 0)) for g in (grad_gate_act, grad_up_act)]
        grad_ffn = scatter_rep(jnp.concatenate(grad_ffn, axis=2))
        grad_attn = (BRANCH_SCALE * grad_middle).astype(BF16)
        grad_mixed = exchange(by_heads(mm(out_w, grad_attn, 1, 1).astype(BF16)))
        grad_attn_cols = after(grad_attn.T.reshape(n, depth, rows), grad_mixed)
        grad_attn_cols = exchange(grad_attn_cols).transpose(1, 0, 2).reshape(depth, all_rows)
        grad_mixed = grad_mixed.transpose(1, 0, 2).reshape(block, all_rows)
        grad_qkv = attend_back(
            base, slots, n, rows, qkv, grad_mixed, scale_one, cosine, sine, bias
        )
        grad_ffn = exchange(after(grad_ffn, grad_mixed))
        grad_ffn = grad_ffn.reshape(n, 2, part, cols).transpose(1, 2, 0, 3).reshape(2, part, ff)
        grad_gate, grad_up, grad_gain_two = finish_all(grad_ffn, (w_gate, w_up), gain_two)
        grad_w = jnp.concatenate(
            [
                row_major(mm(inputs, grad_qkv, 0, 1).astype(BF16)),
                row_major(mm(mixed_all, grad_attn_cols, 1, 1).astype(BF16)),
            ],
            axis=1,
        )
        partial = mm(after(grad_qkv, grad_w), qkv_w, 0, 1)
        back_one = scatter_shard(partial.astype(BF16).reshape(n, rows, width))
        my_inputs = tokens.astype(F32)
        my_scale_one = lax.rsqrt(jnp.mean(my_inputs * my_inputs, axis=-1, keepdims=True) + EPSILON)
        my_normed_one = my_inputs * my_scale_one
        inner_mean = jnp.mean(back_one * my_normed_one, axis=-1, keepdims=True)
        input_grad = grad_middle + back_one - my_normed_one * inner_mean

        branch = mm(after(inner, back_two), down_w, 1, 0).astype(BF16).reshape(n, rows, width)
        branch = scatter_shard(after(branch, back_one))
        out_tokens = (my_middle + BRANCH_SCALE * branch).astype(BF16)

        grad_w = exchange(scatter_rep(grad_w.reshape(n, rep, part, -1)))
        grad_w = jnp.stack(
            [from_heads(grad_w, kind) for kind in range(3)]
            + [grad_w[:, :, 3 * block :].transpose(1, 0, 2).reshape(part, width)]
        )
        grad_query, grad_key, grad_value, grad_out, grad_gain_one = finish_all(
            grad_w, (w_query, w_key, w_value), gain_one
        )
        return (
            out_tokens,
            input_grad,
            grad_gain_one.reshape(depth),
            grad_query,
            grad_key,
            grad_value,
            grad_out,
            grad_gain_two.reshape(depth),
            grad_gate,
            grad_up,
            grad_down,
        )

    return local


def solution(mesh):
    tokens = P(("rep", "shard"), None)
    weight = P("shard", None)
    gain = P("shard")
    return jax.shard_map(
        build(mesh.shape["rep"], mesh.shape["shard"]),
        mesh=mesh,
        in_specs=(
            tokens,
            tokens,
            tokens,
            gain,
            weight,
            weight,
            weight,
            weight,
            gain,
            weight,
            weight,
            weight,
            tokens,
        ),
        out_specs=(
            tokens,
            tokens,
            gain,
            weight,
            weight,
            weight,
            weight,
            gain,
            weight,
            weight,
            weight,
        ),
        check_vma=False,
    )
```

```python
import functools
import math

import jax
import jax.numpy as jnp
from jax import lax
from jax.experimental import pallas as pl
from jax.experimental.layout import Layout, with_layout_constraint
from jax.experimental.pallas import tpu as pltpu
from jax.sharding import PartitionSpec as P

HD = 64
HALF = HD // 2
PIC = 64

EPSILON = 1e-05
BRANCH_SCALE = 1.4 / math.sqrt(40.0)
MASKED = -1e30
F32 = jnp.float32
BF16 = jnp.bfloat16


def mm(left, right, left_dim, right_dim):
    return lax.dot_general(
        left, right, (((left_dim,), (right_dim,)), ((), ())), preferred_element_type=F32
    )


def layout(lengths, starts, row_count):
    places = jnp.arange(row_count, dtype=jnp.int32)
    bounds = jnp.cumsum(lengths)
    firsts = bounds - lengths
    member = (places[:, None] >= firsts[None, :]) & (places[:, None] < bounds[None, :])
    doc_of = jnp.sum(
        jnp.where(member, jnp.arange(lengths.shape[0], dtype=jnp.int32)[None, :], 0), axis=1
    )
    starting = jnp.sum(jnp.where(member, firsts[None, :], 0), axis=1)
    inside = (places[None, :] >= starts[:, None]) & (places[None, :] < starts[:, None] + PIC)
    shared = jnp.any(inside[:, :, None] & inside[:, None, :], axis=0)
    causal = places[None, :] >= places[:, None]
    allowed = (doc_of[:, None] == doc_of[None, :]) & (causal | shared)
    return (places - starting, allowed)


def turn(values, cosine, sine):
    first, second = values[:HALF], values[HALF:]
    return jnp.concatenate([first * cosine - second * sine, second * cosine + first * sine], axis=0)


def probabilities(keys, query, bias):
    scores = mm(keys, query, 0, 0) * HD**-0.5 + bias
    expo = jnp.exp(scores - jnp.max(scores, axis=0, keepdims=True))
    return expo / jnp.sum(expo, axis=0, keepdims=True)


def feature_rows(base, slots, kind, head):
    if head < base:
        return (kind * base + head) * HD
    return (3 * base + kind * (slots - base) + head - base) * HD


def attend_kernel(base, slots, qkv_ref, scale_ref, cos_ref, sin_ref, bias_ref, qkv_out_ref, mixed_ref):
    scale = scale_ref[...]
    cosine, sine, bias = cos_ref[...], sin_ref[...], bias_ref[0]
    for head in range(slots):
        at = [pl.ds(feature_rows(base, slots, kind, head), HD) for kind in range(3)]
        query = turn(qkv_ref[at[0], :] * scale, cosine, sine).astype(BF16)
        keys = turn(qkv_ref[at[1], :] * scale, cosine, sine).astype(BF16)
        values = (qkv_ref[at[2], :] * scale).astype(BF16)
        qkv_out_ref[at[0], :] = query
        qkv_out_ref[at[1], :] = keys
        qkv_out_ref[at[2], :] = values
        probs = probabilities(keys, query, bias).astype(BF16)
        mixed_ref[pl.ds(head * HD, HD), :] = mm(values, probs, 1, 0).astype(BF16)


def attend_back_kernel(base, slots, qkv_ref, grad_ref, scale_ref, cos_ref, sin_ref, bias_ref, out_ref):
    scale = scale_ref[...]
    cosine, sine, bias = cos_ref[...], sin_ref[...], bias_ref[0]
    back = scale * HD**-0.5
    for head in range(slots):
        at = [pl.ds(feature_rows(base, slots, kind, head), HD) for kind in range(3)]
        query = qkv_ref[at[0], :]
        keys = qkv_ref[at[1], :]
        values = qkv_ref[at[2], :]
        grad = grad_ref[pl.ds(head * HD, HD), :]
        probs = probabilities(keys, query, bias)
        grad_values = mm(grad, probs.astype(BF16), 1, 1)
        grad_probs = mm(values, grad, 0, 0)
        inner = jnp.sum(probs * grad_probs, axis=0, keepdims=True)
        grad_scores = (probs * (grad_probs - inner)).astype(BF16)
        grad_query = turn(mm(keys, grad_scores, 1, 0) * back, cosine, -sine)
        grad_keys = turn(mm(query, grad_scores, 1, 1) * back, cosine, -sine)
        out_ref[at[0], :] = grad_query.astype(BF16)
        out_ref[at[1], :] = grad_keys.astype(BF16)
        out_ref[at[2], :] = (grad_values * scale).astype(BF16)


def columns(height, rows):
    return pl.BlockSpec((height, rows), lambda r: (0, r))


def attention_specs(rows):
    return [
        columns(1, rows),
        columns(HALF, rows),
        columns(HALF, rows),
        pl.BlockSpec((1, rows, rows), lambda r: (r, 0, 0)),
    ]


def attend(base, slots, n, rows, qkv, scale, cosine, sine, bias):
    block = slots * HD
    tokens = n * rows
    flops = 4 * n * slots * rows * rows * HD
    return pl.pallas_call(
        functools.partial(attend_kernel, base, slots),
        grid=(n,),
        in_specs=[columns(3 * block, rows)] + attention_specs(rows),
        out_specs=[columns(3 * block, rows), columns(block, rows)],
        out_shape=[
            jax.ShapeDtypeStruct((3 * block, tokens), BF16),
            jax.ShapeDtypeStruct((block, tokens), BF16),
        ],
        cost_estimate=pl.CostEstimate(
            flops=flops, bytes_accessed=20 * block * tokens, transcendentals=n * slots * rows * rows
        ),
        compiler_params=pltpu.CompilerParams(vmem_limit_bytes=12 * 2**20),
        name="attend",
    )(qkv, scale, cosine, sine, bias)


def attend_back(base, slots, n, rows, qkv, grad, scale, cosine, sine, bias):
    block = slots * HD
    tokens = n * rows
    flops = 10 * n * slots * rows * rows * HD
    return pl.pallas_call(
        functools.partial(attend_back_kernel, base, slots),
        grid=(n,),
        in_specs=[columns(3 * block, rows), columns(block, rows)] + attention_specs(rows),
        out_specs=columns(3 * block, rows),
        out_shape=jax.ShapeDtypeStruct((3 * block, tokens), BF16),
        cost_estimate=pl.CostEstimate(
            flops=flops, bytes_accessed=14 * block * tokens, transcendentals=n * slots * rows * rows
        ),
        compiler_params=pltpu.CompilerParams(vmem_limit_bytes=16 * 2**20),
        name="attend_back",
    )(qkv, grad, scale, cosine, sine, bias)


def middle_kernel(me_ref, mixed_ref, weight_ref, inputs_ref, low_ref, scale_ref, own_ref):
    branch = mm(mixed_ref[...], weight_ref[...], 0, 0)
    middle = inputs_ref[...].astype(F32) + BRANCH_SCALE * branch
    scale = lax.rsqrt(jnp.mean(middle * middle, axis=1, keepdims=True) + EPSILON)
    low_ref[...] = middle.astype(BF16)
    scale_ref[...] = scale

    @pl.when(pl.program_id(0) == me_ref[0])
    def _():
        own_ref[...] = middle


def middle_rows(me, mixed, weight, inputs, rows):
    tokens, width = inputs.shape
    return pl.pallas_call(
        middle_kernel,
        grid_spec=pltpu.PrefetchScalarGridSpec(
            num_scalar_prefetch=1,
            grid=(tokens // rows,),
            in_specs=[
                pl.BlockSpec((width, rows), lambda i, me: (0, i)),
                pl.BlockSpec((width, width), lambda i, me: (0, 0), pipeline_mode=pl.Buffered(1)),
                pl.BlockSpec((rows, width), lambda i, me: (i, 0)),
            ],
            out_specs=[
                pl.BlockSpec((rows, width), lambda i, me: (i, 0)),
                pl.BlockSpec((rows, 1), lambda i, me: (i, 0)),
                pl.BlockSpec((rows, width), lambda i, me: (0, 0)),
            ],
        ),
        out_shape=[
            jax.ShapeDtypeStruct((tokens, width), BF16),
            jax.ShapeDtypeStruct((tokens, 1), F32),
            jax.ShapeDtypeStruct((rows, width), F32),
        ],
        cost_estimate=pl.CostEstimate(
            flops=2 * tokens * width * width,
            bytes_accessed=2 * width * width + 6 * tokens * width,
            transcendentals=tokens,
        ),
        compiler_params=pltpu.CompilerParams(vmem_limit_bytes=40 * 2**20),
        name="middle_rows",
    )(me.reshape(1), mixed, weight, inputs)


def row_major(array):
    return with_layout_constraint(array, Layout(tuple(range(array.ndim))))


def empty(shape, dtype):
    return pl.pallas_call(
        lambda out_ref: None,
        out_specs=pl.BlockSpec(memory_space=pl.ANY),
        out_shape=jax.ShapeDtypeStruct(shape, dtype),
        compiler_params=pltpu.CompilerParams(vmem_limit_bytes=1 * 2**20),
        name="empty",
    )()


def low(weight):
    return weight.astype(BF16).astype(F32)


def prepare_kernel(n, base, slots, heads, own_ref, query_ref, key_ref, value_ref, gain_ref, info_ref, out_ref):
    part = query_ref.shape[1]
    main = base * HD
    for kind, ref in enumerate((query_ref, key_ref, value_ref)):
        weight = (low(ref[0]) * gain_ref[0]).astype(BF16)
        for j in range(n):
            out_ref[j, :part, kind * main : (kind + 1) * main] = weight[:, j * main : (j + 1) * main]
            if slots > base:
                first = 3 * main + kind * HD
                head = n * base + j
                if head < heads:
                    extra = weight[:, head * HD : (head + 1) * HD]
                else:
                    extra = jnp.zeros((part, HD), BF16)
                out_ref[j, :part, first : first + HD] = extra
    for j in range(n):
        out_ref[j, part:, :] = info_ref[...]


def prepare_ffn_kernel(n, own_ref, gate_ref, up_ref, gain_ref, out_ref):
    part, cols = gate_ref.shape[1], out_ref.shape[2]
    for kind, ref in enumerate((gate_ref, up_ref)):
        weight = (low(ref[0]) * gain_ref[0]).astype(BF16)
        for j in range(n):
            out_ref[j, kind * part : (kind + 1) * part, :] = weight[:, j * cols : (j + 1) * cols]


def own_part(part, width):
    return pl.BlockSpec((1, part, width), lambda i, own: (own[0], 0, 0))


def prepare(kernel, own, weights, gain, more, out_shape, name):
    part = weights[0].shape[1]
    return pl.pallas_call(
        kernel,
        grid_spec=pltpu.PrefetchScalarGridSpec(
            num_scalar_prefetch=1,
            grid=(1,),
            in_specs=[own_part(part, w.shape[2]) for w in weights]
            + [own_part(part, 1)]
            + [pl.BlockSpec(m.shape, lambda i, own: (0, 0)) for m in more],
            out_specs=pl.BlockSpec(out_shape, lambda i, own: (0, 0, 0)),
        ),
        out_shape=jax.ShapeDtypeStruct(out_shape, BF16),
        name=name,
    )(own, *weights, gain, *more)


def finish_kernel(count, gained, at_ref, piece_ref, *refs):
    weights = refs[:gained]
    outs = refs[-(count + (gained > 0)) :]
    total = 0.0
    for k in range(count):
        raw = piece_ref[k].astype(F32)
        if k < gained:
            total = total + jnp.sum(weights[k][0] * raw, axis=1, keepdims=True)
            raw = raw * refs[gained][0]
        outs[k][0] = raw
    if gained:
        first = pl.program_id(0) == 0
        outs[count][0] = jnp.where(first, 0.0, outs[count][0]) + total


def finish(piece, at, rep, weights, gain, previous):
    count, part, width = piece.shape
    gained = len(weights)
    chunk = 1152 if width == 2304 else width

    def placed(size, moving):
        return pl.BlockSpec((1, part, size), lambda i, at: (at[0], 0, i if moving else 0))

    in_specs = [pl.BlockSpec((count, part, chunk), lambda i, at: (0, 0, i))]
    operands = [piece]
    out_specs = [placed(chunk, True)] * count
    out_shape = [jax.ShapeDtypeStruct((rep, part, width), F32)] * count
    if gained:
        in_specs += [placed(chunk, True)] * gained + [placed(1, False)]
        operands += list(weights) + [gain]
        out_specs.append(placed(1, False))
        out_shape.append(jax.ShapeDtypeStruct((rep, part, 1), F32))
    aliases = {}
    if previous is not None:
        aliases = {1 + len(operands) + k: k for k in range(len(out_shape))}
        operands += list(previous)
        in_specs += [pl.BlockSpec(memory_space=pl.ANY)] * len(out_shape)
    return pl.pallas_call(
        functools.partial(finish_kernel, count, gained),
        grid_spec=pltpu.PrefetchScalarGridSpec(
            num_scalar_prefetch=1, grid=(width // chunk,), in_specs=in_specs, out_specs=out_specs
        ),
        out_shape=out_shape,
        input_output_aliases=aliases,
        cost_estimate=pl.CostEstimate(
            flops=4 * count * part * width,
            bytes_accessed=(6 * count + 4 * gained) * part * width,
            transcendentals=0,
        ),
        name="finish",
    )(at, *operands)


def build(rep, n):
    cycle = list(range(0, n, 2)) + list(range(n - 1, 0, -2)) if n % 2 == 0 else list(range(n))
    to_right = [(cycle[i], cycle[(i + 1) % n]) for i in range(n)]
    to_left = [(b, a) for a, b in to_right]
    steps_right = n // 2
    steps_left = n - 1 - steps_right
    outer = rep // 2
    core_pairs = [(i, i ^ 1) for i in range(rep)]
    chip_pairs = [(i, (i + 2) % rep) for i in range(rep)]

    def right(x):
        return lax.ppermute(x, "shard", to_right)

    def left(x):
        return lax.ppermute(x, "shard", to_left)

    def core_swap(x):
        return lax.ppermute(x, "rep", core_pairs)

    def chip_swap(x):
        return lax.ppermute(x, "rep", chip_pairs)

    def ring_device(offset):
        device = lax.axis_index("shard")
        if n % 2:
            return (device + offset + n) % n
        place = jnp.where(device % 2 == 0, device // 2, n - 1 - device // 2)
        place = (place + offset + n) % n
        return jnp.where(place < n // 2, 2 * place, 2 * (n - 1 - place) + 1)

    def after(value, *others):
        return lax.optimization_barrier((value, others))[0]

    def ring_gather(piece, gates=(), paired=False):
        pieces = [(ring_device(0), piece)]
        going_right = going_left = piece
        for step in range(1, steps_right + 1):
            if step <= len(gates) and gates[step - 1] is not None:
                going_right, going_left = after((going_right, going_left), gates[step - 1])
            going_right = right(going_right)
            if step <= steps_left:
                going_left = left(going_left)
                if paired:
                    going_right, going_left = lax.optimization_barrier((going_right, going_left))
                pieces.append((ring_device(step), going_left))
            pieces.append((ring_device(-step), going_right))
        return pieces

    def assemble(pieces):
        shape = pieces[0][1].shape
        whole = empty((n,) + shape, pieces[0][1].dtype)
        for device, part in pieces:
            whole = lax.dynamic_update_index_in_dim(whole, part, device, 0)
        return whole.reshape((-1,) + shape[1:])

    def scatter_shard(parts, gates=()):
        def term(offset):
            return lax.dynamic_index_in_dim(parts, ring_device(offset), 0, keepdims=False).astype(F32)

        going_right = term(steps_right).astype(BF16)
        going_left = term(-steps_left).astype(BF16)
        for step in range(1, steps_right + 1):
            if step <= len(gates) and gates[step - 1] is not None:
                going_right, going_left = after((going_right, going_left), gates[step - 1])
            going_right = right(going_right)
            if step < steps_right:
                going_right = (going_right.astype(F32) + term(steps_right - step)).astype(BF16)
            if step <= steps_left:
                going_left = left(going_left)
                if step < steps_left:
                    going_left = (going_left.astype(F32) + term(step - steps_left)).astype(BF16)
        return going_right.astype(F32) + going_left.astype(F32) + term(0)

    def exchange(blocks):
        return lax.all_to_all(blocks, "shard", split_axis=0, concat_axis=0, tiled=True)

    def pick(array, index, axis):
        return lax.dynamic_index_in_dim(array, index, axis, keepdims=False)

    def add(a, b):
        return (a.astype(F32) + b.astype(F32)).astype(BF16)

    def rep_pieces(piece):
        mine = lax.axis_index("rep")
        far = (mine + 2) % rep
        other_chip = chip_swap(piece)
        other_core = core_swap(piece)
        last = core_swap(other_chip)
        return [(mine, piece), (mine ^ 1, other_core), (far, other_chip), (far ^ 1, last)]

    def gather_rep(piece, axis, pieces=None):
        whole = empty(piece.shape[:axis] + (rep,) + piece.shape[axis:], piece.dtype)
        for index, part in rep_pieces(piece) if pieces is None else pieces:
            whole = lax.dynamic_update_index_in_dim(whole, part, index, axis)
        return whole

    def scatter_rep(blocks):
        mine = lax.axis_index("rep")
        chip, core = mine // 2, mine % 2
        blocks = blocks.reshape((blocks.shape[0], outer, 2) + blocks.shape[2:])
        half = add(pick(blocks, core, 2), core_swap(pick(blocks, 1 - core, 2)))
        return add(pick(half, chip, 1), chip_swap(pick(half, 1 - chip, 1)))

    def local(
        tokens,
        doc_lengths,
        pic_starts,
        attn_gain,
        w_query,
        w_key,
        w_value,
        w_out,
        ffn_gain,
        w_gate,
        w_up,
        w_down,
        cotangent,
    ):
        rows, width = tokens.shape
        heads = width // HD
        base = heads // n
        slots = -(-heads // n)
        block = slots * HD
        main = base * HD
        mains = n * main
        over = heads - n * base
        depth = w_query.shape[0]
        part = depth // rep
        ff = w_gate.shape[1]
        cols = ff // n
        all_rows = n * rows
        me = lax.axis_index("shard")
        mine = lax.axis_index("rep")
        own = mine.reshape(1)
        docs = doc_lengths.shape[1]
        pics = pic_starts.shape[1]

        def by_rep(array):
            return array.reshape(rep, -1, array.shape[1])

        gain_one = by_rep(low(attn_gain)[:, None])
        gain_two = by_rep(low(ffn_gain)[:, None])

        def by_heads(array):
            first = array[:mains].reshape(n, main, -1)
            if slots == base:
                return first
            rest = jnp.pad(array[mains:], ((0, n * HD - (width - mains)), (0, 0)))
            return jnp.concatenate([first, rest.reshape(n, HD, -1)], axis=1)

        def from_heads(array, kind):
            first = array[:, :, kind * main : (kind + 1) * main].transpose(1, 0, 2)
            first = first.reshape(array.shape[1], mains)
            if slots == base:
                return first
            start = 3 * main + kind * HD
            rest = array[:over, :, start : start + HD].transpose(1, 0, 2)
            return jnp.concatenate([first, rest.reshape(array.shape[1], width - mains)], axis=1)

        info = jnp.concatenate([doc_lengths[0], pic_starts[0]]).astype(BF16)
        info = jnp.zeros((8, 3 * block), BF16).at[0, : docs + pics].set(info)
        qkv_part = prepare(
            functools.partial(prepare_kernel, n, base, slots, heads),
            own,
            [by_rep(w) for w in (w_query, w_key, w_value)],
            gain_one,
            [info],
            (n, part + 8, 3 * block),
            "prepare_qkv",
        )
        ffn_part = prepare(
            functools.partial(prepare_ffn_kernel, n),
            own,
            [by_rep(w) for w in (w_gate, w_up)],
            gain_two,
            [],
            (n, 2 * part, cols),
            "prepare_ffn",
        )
        qkv_part = exchange(qkv_part)
        x_pieces = ring_gather(tokens, (None, (qkv_part, ffn_part)), True)
        info = qkv_part[:, part, : docs + pics].astype(jnp.int32)
        near = x_pieces[-2][1]
        out_part = after(pick(by_rep(w_out), mine, 0), near).astype(BF16)
        out_w = lax.all_gather(out_part, ("shard", "rep"), axis=0, tiled=True)
        ffn_part = exchange(after(ffn_part, near))
        qkv_part = qkv_part[:, :part]
        last, qkv_chip = lax.optimization_barrier((x_pieces[-1][1], chip_swap(qkv_part)))
        x_pieces[-1] = (x_pieces[-1][0], last)
        inputs = assemble(x_pieces)
        far = (mine + 2) % rep
        qkv_pieces = [
            (mine, qkv_part),
            (mine ^ 1, core_swap(qkv_part)),
            (far, qkv_chip),
            (far ^ 1, core_swap(qkv_chip)),
        ]
        qkv_w = gather_rep(qkv_part, 1, qkv_pieces).reshape(width, 3 * block)
        down_w = w_down.astype(BF16)
        grad_result = cotangent.astype(F32)

        offsets, allowed = jax.vmap(lambda a, b: layout(a, b, rows))(info[:, :docs], info[:, docs:])
        bias = jnp.where(allowed, 0.0, MASKED).astype(F32)
        freq_table = jnp.exp(jnp.arange(HALF, dtype=F32) * (-2.0 * math.log(10000.0) / HD))
        turned = freq_table[:, None] * offsets.reshape(1, all_rows).astype(F32)
        cosine, sine = jnp.cos(turned), jnp.sin(turned)
        squares = jnp.mean(jnp.square(inputs.astype(F32)), axis=-1)
        scale_one = lax.rsqrt(squares + EPSILON)[None, :]
        qkv = mm(qkv_w, inputs, 0, 1)
        qkv, mixed = attend(base, slots, n, rows, qkv, scale_one, cosine, sine, bias)
        ffn_part = after(ffn_part, mixed)
        ffn_pieces = rep_pieces(ffn_part)
        gate_w, up_w = (
            gather_rep(
                ffn_part[:, k * part : (k + 1) * part],
                1,
                [(at, piece[:, k * part : (k + 1) * part]) for at, piece in ffn_pieces],
            ).reshape(width, cols)
            for k in range(2)
        )
        mixed_all = empty((n * block, all_rows), BF16)
        mixed_pieces = ring_gather(mixed, (), True)
        for device, piece in mixed_pieces:
            mixed_all = lax.dynamic_update_slice_in_dim(mixed_all, piece[:main], device * main, 0)
            if slots > base:
                mixed_all = lax.dynamic_update_slice_in_dim(
                    mixed_all, piece[main:], mains + device * HD, 0
                )
        middle_low, scale_two, my_middle = middle_rows(me, mixed_all, out_w, inputs, rows)

        gate_act = mm(middle_low, gate_w, 1, 0) * scale_two
        up_act = mm(middle_low, up_w, 1, 0) * scale_two
        sigmoid_gate = jax.nn.sigmoid(gate_act)
        silu_gate = gate_act * sigmoid_gate
        inner = (silu_gate * up_act).astype(BF16)
        grad_branch = (BRANCH_SCALE * grad_result).astype(BF16)
        grad_branch = assemble(ring_gather(grad_branch, (mixed_pieces[-1][1], scale_two, up_act)))
        grad_inner = mm(grad_branch, down_w, 1, 1)
        grad_gate_act = (
            grad_inner
            * up_act
            * sigmoid_gate
            * (1.0 + gate_act * (1.0 - sigmoid_gate))
            * scale_two
        ).astype(BF16)
        grad_up_act = (grad_inner * silu_gate * scale_two).astype(BF16)
        partial = mm(grad_gate_act, gate_w, 1, 1) + mm(grad_up_act, up_w, 1, 1)
        partial = partial.astype(BF16).reshape(n, rows, width)
        back_two = scatter_shard(partial)
        my_normed_two = my_middle * lax.dynamic_slice_in_dim(scale_two, me * rows, rows, 0)
        inner_mean = jnp.mean(back_two * my_normed_two, axis=-1, keepdims=True)
        grad_middle = grad_result + back_two - my_normed_two * inner_mean

        def rep_rows(grad):
            return row_major(grad.astype(BF16)).reshape(n, rep, part, grad.shape[1])

        def finish_some(pieces, weights, gain, done):
            for index, arrived in pieces:
                done = finish(
                    arrived, index.reshape(1), rep, [by_rep(w) for w in weights], gain, done
                )
            return done

        def finish_all(piece, weights, gain):
            done = finish_some(rep_pieces(piece), weights, gain, None)
            return [a.reshape(-1, a.shape[2]) for a in done]

        inner, grad_gate_act, grad_up_act, _ = lax.optimization_barrier(
            (inner, grad_gate_act, grad_up_act, partial)
        )
        grad_down = mm(inner, grad_branch, 0, 0).astype(BF16).reshape(1, rep, -1, width)
        (grad_down,) = finish_all(scatter_rep(grad_down), (), None)
        grad_ffn = [rep_rows(mm(middle_low, g, 0, 0)) for g in (grad_gate_act, grad_up_act)]
        grad_ffn = scatter_rep(jnp.concatenate(grad_ffn, axis=2))
        grad_attn = (BRANCH_SCALE * grad_middle).astype(BF16)
        both = exchange(
            jnp.concatenate(
                [
                    by_heads(mm(out_w, grad_attn, 1, 1).astype(BF16)),
                    grad_attn.T.reshape(n, depth, rows),
                ],
                axis=1,
            )
        )
        grad_mixed = both[:, :block].transpose(1, 0, 2).reshape(block, all_rows)
        grad_attn_cols = both[:, block:].transpose(1, 0, 2).reshape(depth, all_rows)
        grad_qkv = attend_back(
            base, slots, n, rows, qkv, grad_mixed, scale_one, cosine, sine, bias
        )
        grad_w = jnp.concatenate(
            [
                row_major(mm(inputs, grad_qkv, 0, 1).astype(BF16)),
                row_major(mm(mixed_all, after(grad_attn_cols, grad_qkv), 1, 1).astype(BF16))[:width],
            ],
            axis=1,
        )
        grad_w, grad_ffn = lax.optimization_barrier((grad_w, grad_ffn))
        grad_ffn = exchange(grad_ffn)
        partial = mm(after(grad_qkv, grad_w), qkv_w, 0, 1)
        ffn_blocks = grad_ffn
        grad_ffn = grad_ffn.reshape(n, 2, part, cols).transpose(1, 2, 0, 3).reshape(2, part, ff)
        back_one = scatter_shard(
            partial.astype(BF16).reshape(n, rows, width), (None, None, ffn_blocks)
        )
        ffn_pieces = rep_pieces(grad_ffn)
        ffn_half = finish_some(ffn_pieces[:2], (w_gate, w_up), gain_two, None)
        ffn_done = finish_some(ffn_pieces[2:], (w_gate, w_up), gain_two, ffn_half)
        grad_gate, grad_up, grad_gain_two = (a.reshape(-1, a.shape[2]) for a in ffn_done)
        my_inputs = tokens.astype(F32)
        my_scale_one = lax.rsqrt(jnp.mean(my_inputs * my_inputs, axis=-1, keepdims=True) + EPSILON)
        my_normed_one = my_inputs * my_scale_one
        inner_mean = jnp.mean(back_one * my_normed_one, axis=-1, keepdims=True)
        input_grad = grad_middle + back_one - my_normed_one * inner_mean

        branch = mm(after(inner, back_two), down_w, 1, 0).astype(BF16).reshape(n, rows, width)
        branch = scatter_shard(after(branch, back_one), (None, grad_down, None, ffn_half))
        out_tokens = (my_middle + BRANCH_SCALE * branch).astype(BF16)

        grad_w = exchange(scatter_rep(grad_w.reshape(n, rep, part, -1)))
        grad_w = jnp.stack(
            [from_heads(grad_w, kind) for kind in range(3)]
            + [grad_w[:, :, 3 * block :].transpose(1, 0, 2).reshape(part, width)]
        )
        grad_query, grad_key, grad_value, grad_out, grad_gain_one = finish_all(
            grad_w, (w_query, w_key, w_value), gain_one
        )
        return (
            out_tokens,
            input_grad,
            grad_gain_one.reshape(depth),
            grad_query,
            grad_key,
            grad_value,
            grad_out,
            grad_gain_two.reshape(depth),
            grad_gate,
            grad_up,
            grad_down,
        )

    return local


def solution(mesh):
    tokens = P(("rep", "shard"), None)
    weight = P("shard", None)
    gain = P("shard")
    return jax.shard_map(
        build(mesh.shape["rep"], mesh.shape["shard"]),
        mesh=mesh,
        in_specs=(
            tokens,
            tokens,
            tokens,
            gain,
            weight,
            weight,
            weight,
            weight,
            gain,
            weight,
            weight,
            weight,
            tokens,
        ),
        out_specs=(
            tokens,
            tokens,
            gain,
            weight,
            weight,
            weight,
            weight,
            gain,
            weight,
            weight,
            weight,
        ),
        check_vma=False,
    )
```

```python
import functools
import math

import jax
import jax.numpy as jnp
from jax import lax
from jax.experimental import pallas as pl
from jax.experimental.layout import Layout, with_layout_constraint
from jax.experimental.pallas import tpu as pltpu
from jax.sharding import PartitionSpec as P

HD = 64
HALF = HD // 2
PIC = 64

EPSILON = 1e-05
BRANCH_SCALE = 1.4 / math.sqrt(40.0)
MASKED = -1e30
F32 = jnp.float32
BF16 = jnp.bfloat16


def mm(left, right, left_dim, right_dim):
    return lax.dot_general(
        left, right, (((left_dim,), (right_dim,)), ((), ())), preferred_element_type=F32
    )


def layout(lengths, starts, row_count):
    places = jnp.arange(row_count, dtype=jnp.int32)
    bounds = jnp.cumsum(lengths)
    firsts = bounds - lengths
    member = (places[:, None] >= firsts[None, :]) & (places[:, None] < bounds[None, :])
    doc_of = jnp.sum(
        jnp.where(member, jnp.arange(lengths.shape[0], dtype=jnp.int32)[None, :], 0), axis=1
    )
    starting = jnp.sum(jnp.where(member, firsts[None, :], 0), axis=1)
    inside = (places[None, :] >= starts[:, None]) & (places[None, :] < starts[:, None] + PIC)
    shared = jnp.any(inside[:, :, None] & inside[:, None, :], axis=0)
    causal = places[None, :] >= places[:, None]
    allowed = (doc_of[:, None] == doc_of[None, :]) & (causal | shared)
    return (places - starting, allowed)


def turn(values, cosine, sine):
    first, second = values[:HALF], values[HALF:]
    return jnp.concatenate([first * cosine - second * sine, second * cosine + first * sine], axis=0)


def probabilities(keys, query, bias):
    scores = mm(keys, query, 0, 0) * HD**-0.5 + bias
    expo = jnp.exp(scores - jnp.max(scores, axis=0, keepdims=True))
    return expo / jnp.sum(expo, axis=0, keepdims=True)


def feature_rows(base, slots, kind, head):
    if head < base:
        return (kind * base + head) * HD
    return (3 * base + kind * (slots - base) + head - base) * HD


def attend_kernel(base, slots, qkv_ref, scale_ref, cos_ref, sin_ref, bias_ref, qkv_out_ref, mixed_ref):
    scale = scale_ref[...]
    cosine, sine, bias = cos_ref[...], sin_ref[...], bias_ref[0]
    for head in range(slots):
        at = [pl.ds(feature_rows(base, slots, kind, head), HD) for kind in range(3)]
        query = turn(qkv_ref[at[0], :] * scale, cosine, sine).astype(BF16)
        keys = turn(qkv_ref[at[1], :] * scale, cosine, sine).astype(BF16)
        values = (qkv_ref[at[2], :] * scale).astype(BF16)
        qkv_out_ref[at[0], :] = query
        qkv_out_ref[at[1], :] = keys
        qkv_out_ref[at[2], :] = values
        probs = probabilities(keys, query, bias).astype(BF16)
        mixed_ref[pl.ds(head * HD, HD), :] = mm(values, probs, 1, 0).astype(BF16)


def attend_back_kernel(base, slots, qkv_ref, grad_ref, scale_ref, cos_ref, sin_ref, bias_ref, out_ref):
    scale = scale_ref[...]
    cosine, sine, bias = cos_ref[...], sin_ref[...], bias_ref[0]
    back = scale * HD**-0.5
    for head in range(slots):
        at = [pl.ds(feature_rows(base, slots, kind, head), HD) for kind in range(3)]
        query = qkv_ref[at[0], :]
        keys = qkv_ref[at[1], :]
        values = qkv_ref[at[2], :]
        grad = grad_ref[pl.ds(head * HD, HD), :]
        probs = probabilities(keys, query, bias)
        grad_values = mm(grad, probs.astype(BF16), 1, 1)
        grad_probs = mm(values, grad, 0, 0)
        inner = jnp.sum(probs * grad_probs, axis=0, keepdims=True)
        grad_scores = (probs * (grad_probs - inner)).astype(BF16)
        grad_query = turn(mm(keys, grad_scores, 1, 0) * back, cosine, -sine)
        grad_keys = turn(mm(query, grad_scores, 1, 1) * back, cosine, -sine)
        out_ref[at[0], :] = grad_query.astype(BF16)
        out_ref[at[1], :] = grad_keys.astype(BF16)
        out_ref[at[2], :] = (grad_values * scale).astype(BF16)


def columns(height, rows):
    return pl.BlockSpec((height, rows), lambda r: (0, r))


def attention_specs(rows):
    return [
        columns(1, rows),
        columns(HALF, rows),
        columns(HALF, rows),
        pl.BlockSpec((1, rows, rows), lambda r: (r, 0, 0)),
    ]


def attend(base, slots, n, rows, qkv, scale, cosine, sine, bias):
    block = slots * HD
    tokens = n * rows
    flops = 4 * n * slots * rows * rows * HD
    return pl.pallas_call(
        functools.partial(attend_kernel, base, slots),
        grid=(n,),
        in_specs=[columns(3 * block, rows)] + attention_specs(rows),
        out_specs=[columns(3 * block, rows), columns(block, rows)],
        out_shape=[
            jax.ShapeDtypeStruct((3 * block, tokens), BF16),
            jax.ShapeDtypeStruct((block, tokens), BF16),
        ],
        cost_estimate=pl.CostEstimate(
            flops=flops, bytes_accessed=20 * block * tokens, transcendentals=n * slots * rows * rows
        ),
        compiler_params=pltpu.CompilerParams(vmem_limit_bytes=12 * 2**20),
        name="attend",
    )(qkv, scale, cosine, sine, bias)


def attend_back(base, slots, n, rows, qkv, grad, scale, cosine, sine, bias):
    block = slots * HD
    tokens = n * rows
    flops = 10 * n * slots * rows * rows * HD
    return pl.pallas_call(
        functools.partial(attend_back_kernel, base, slots),
        grid=(n,),
        in_specs=[columns(3 * block, rows), columns(block, rows)] + attention_specs(rows),
        out_specs=columns(3 * block, rows),
        out_shape=jax.ShapeDtypeStruct((3 * block, tokens), BF16),
        cost_estimate=pl.CostEstimate(
            flops=flops, bytes_accessed=14 * block * tokens, transcendentals=n * slots * rows * rows
        ),
        compiler_params=pltpu.CompilerParams(vmem_limit_bytes=16 * 2**20),
        name="attend_back",
    )(qkv, grad, scale, cosine, sine, bias)


def middle_kernel(me_ref, mixed_ref, weight_ref, inputs_ref, low_ref, scale_ref, own_ref):
    branch = mm(mixed_ref[...], weight_ref[...], 0, 0)
    middle = inputs_ref[...].astype(F32) + BRANCH_SCALE * branch
    scale = lax.rsqrt(jnp.mean(middle * middle, axis=1, keepdims=True) + EPSILON)
    low_ref[...] = middle.astype(BF16)
    scale_ref[...] = scale

    @pl.when(pl.program_id(0) == me_ref[0])
    def _():
        own_ref[...] = middle


def middle_rows(me, mixed, weight, inputs, rows):
    tokens, width = inputs.shape
    return pl.pallas_call(
        middle_kernel,
        grid_spec=pltpu.PrefetchScalarGridSpec(
            num_scalar_prefetch=1,
            grid=(tokens // rows,),
            in_specs=[
                pl.BlockSpec((width, rows), lambda i, me: (0, i)),
                pl.BlockSpec((width, width), lambda i, me: (0, 0), pipeline_mode=pl.Buffered(1)),
                pl.BlockSpec((rows, width), lambda i, me: (i, 0)),
            ],
            out_specs=[
                pl.BlockSpec((rows, width), lambda i, me: (i, 0)),
                pl.BlockSpec((rows, 1), lambda i, me: (i, 0)),
                pl.BlockSpec((rows, width), lambda i, me: (0, 0)),
            ],
        ),
        out_shape=[
            jax.ShapeDtypeStruct((tokens, width), BF16),
            jax.ShapeDtypeStruct((tokens, 1), F32),
            jax.ShapeDtypeStruct((rows, width), F32),
        ],
        cost_estimate=pl.CostEstimate(
            flops=2 * tokens * width * width,
            bytes_accessed=2 * width * width + 6 * tokens * width,
            transcendentals=tokens,
        ),
        compiler_params=pltpu.CompilerParams(vmem_limit_bytes=40 * 2**20),
        name="middle_rows",
    )(me.reshape(1), mixed, weight, inputs)


def row_major(array):
    return with_layout_constraint(array, Layout(tuple(range(array.ndim))))


def empty(shape, dtype):
    return pl.pallas_call(
        lambda out_ref: None,
        out_specs=pl.BlockSpec(memory_space=pl.ANY),
        out_shape=jax.ShapeDtypeStruct(shape, dtype),
        compiler_params=pltpu.CompilerParams(vmem_limit_bytes=1 * 2**20),
        name="empty",
    )()


def low(weight):
    return weight.astype(BF16).astype(F32)


def prepare_kernel(n, base, slots, heads, own_ref, query_ref, key_ref, value_ref, gain_ref, info_ref, out_ref):
    part = query_ref.shape[1]
    main = base * HD
    for kind, ref in enumerate((query_ref, key_ref, value_ref)):
        weight = (low(ref[0]) * gain_ref[0]).astype(BF16)
        for j in range(n):
            out_ref[j, :part, kind * main : (kind + 1) * main] = weight[:, j * main : (j + 1) * main]
            if slots > base:
                first = 3 * main + kind * HD
                head = n * base + j
                if head < heads:
                    extra = weight[:, head * HD : (head + 1) * HD]
                else:
                    extra = jnp.zeros((part, HD), BF16)
                out_ref[j, :part, first : first + HD] = extra
    for j in range(n):
        out_ref[j, part:, :] = info_ref[...]


def prepare_ffn_kernel(n, own_ref, gate_ref, up_ref, gain_ref, out_ref):
    part, cols = gate_ref.shape[1], out_ref.shape[2]
    for kind, ref in enumerate((gate_ref, up_ref)):
        weight = (low(ref[0]) * gain_ref[0]).astype(BF16)
        for j in range(n):
            out_ref[j, kind * part : (kind + 1) * part, :] = weight[:, j * cols : (j + 1) * cols]


def own_part(part, width):
    return pl.BlockSpec((1, part, width), lambda i, own: (own[0], 0, 0))


def prepare(kernel, own, weights, gain, more, out_shape, name):
    part = weights[0].shape[1]
    return pl.pallas_call(
        kernel,
        grid_spec=pltpu.PrefetchScalarGridSpec(
            num_scalar_prefetch=1,
            grid=(1,),
            in_specs=[own_part(part, w.shape[2]) for w in weights]
            + [own_part(part, 1)]
            + [pl.BlockSpec(m.shape, lambda i, own: (0, 0)) for m in more],
            out_specs=pl.BlockSpec(out_shape, lambda i, own: (0, 0, 0)),
        ),
        out_shape=jax.ShapeDtypeStruct(out_shape, BF16),
        name=name,
    )(own, *weights, gain, *more)


def finish_kernel(count, gained, at_ref, piece_ref, *refs):
    weights = refs[:gained]
    outs = refs[-(count + (gained > 0)) :]
    total = 0.0
    for k in range(count):
        raw = piece_ref[k].astype(F32)
        if k < gained:
            total = total + jnp.sum(weights[k][0] * raw, axis=1, keepdims=True)
            raw = raw * refs[gained][0]
        outs[k][0] = raw
    if gained:
        first = pl.program_id(0) == 0
        outs[count][0] = jnp.where(first, 0.0, outs[count][0]) + total


def finish(piece, at, rep, weights, gain, previous):
    count, part, width = piece.shape
    gained = len(weights)
    chunk = 1152 if width == 2304 else width

    def placed(size, moving):
        return pl.BlockSpec((1, part, size), lambda i, at: (at[0], 0, i if moving else 0))

    in_specs = [pl.BlockSpec((count, part, chunk), lambda i, at: (0, 0, i))]
    operands = [piece]
    out_specs = [placed(chunk, True)] * count
    out_shape = [jax.ShapeDtypeStruct((rep, part, width), F32)] * count
    if gained:
        in_specs += [placed(chunk, True)] * gained + [placed(1, False)]
        operands += list(weights) + [gain]
        out_specs.append(placed(1, False))
        out_shape.append(jax.ShapeDtypeStruct((rep, part, 1), F32))
    aliases = {}
    if previous is not None:
        aliases = {1 + len(operands) + k: k for k in range(len(out_shape))}
        operands += list(previous)
        in_specs += [pl.BlockSpec(memory_space=pl.ANY)] * len(out_shape)
    return pl.pallas_call(
        functools.partial(finish_kernel, count, gained),
        grid_spec=pltpu.PrefetchScalarGridSpec(
            num_scalar_prefetch=1, grid=(width // chunk,), in_specs=in_specs, out_specs=out_specs
        ),
        out_shape=out_shape,
        input_output_aliases=aliases,
        cost_estimate=pl.CostEstimate(
            flops=4 * count * part * width,
            bytes_accessed=(6 * count + 4 * gained) * part * width,
            transcendentals=0,
        ),
        name="finish",
    )(at, *operands)


def build(rep, n):
    cycle = list(range(0, n, 2)) + list(range(n - 1, 0, -2)) if n % 2 == 0 else list(range(n))
    to_right = [(cycle[i], cycle[(i + 1) % n]) for i in range(n)]
    to_left = [(b, a) for a, b in to_right]
    steps_right = n // 2
    steps_left = n - 1 - steps_right
    outer = rep // 2
    core_pairs = [(i, i ^ 1) for i in range(rep)]
    chip_pairs = [(i, (i + 2) % rep) for i in range(rep)]

    def right(x):
        return lax.ppermute(x, "shard", to_right)

    def left(x):
        return lax.ppermute(x, "shard", to_left)

    def core_swap(x):
        return lax.ppermute(x, "rep", core_pairs)

    def chip_swap(x):
        return lax.ppermute(x, "rep", chip_pairs)

    def ring_device(offset):
        device = lax.axis_index("shard")
        if n % 2:
            return (device + offset + n) % n
        place = jnp.where(device % 2 == 0, device // 2, n - 1 - device // 2)
        place = (place + offset + n) % n
        return jnp.where(place < n // 2, 2 * place, 2 * (n - 1 - place) + 1)

    def after(value, *others):
        return lax.optimization_barrier((value, others))[0]

    def ring_gather(piece, gates=(), paired=False):
        pieces = [(ring_device(0), piece)]
        going_right = going_left = piece
        for step in range(1, steps_right + 1):
            if step <= len(gates) and gates[step - 1] is not None:
                going_right, going_left = after((going_right, going_left), gates[step - 1])
            going_right = right(going_right)
            if step <= steps_left:
                going_left = left(going_left)
                if paired:
                    going_right, going_left = lax.optimization_barrier((going_right, going_left))
                pieces.append((ring_device(step), going_left))
            pieces.append((ring_device(-step), going_right))
        return pieces

    def assemble(pieces):
        shape = pieces[0][1].shape
        whole = empty((n,) + shape, pieces[0][1].dtype)
        for device, part in pieces:
            whole = lax.dynamic_update_index_in_dim(whole, part, device, 0)
        return whole.reshape((-1,) + shape[1:])

    def scatter_shard(parts, gates=()):
        def term(offset):
            return lax.dynamic_index_in_dim(parts, ring_device(offset), 0, keepdims=False).astype(F32)

        going_right = term(steps_right).astype(BF16)
        going_left = term(-steps_left).astype(BF16)
        for step in range(1, steps_right + 1):
            if step <= len(gates) and gates[step - 1] is not None:
                going_right, going_left = after((going_right, going_left), gates[step - 1])
            going_right = right(going_right)
            if step < steps_right:
                going_right = (going_right.astype(F32) + term(steps_right - step)).astype(BF16)
            if step <= steps_left:
                going_left = left(going_left)
                if step < steps_left:
                    going_left = (going_left.astype(F32) + term(step - steps_left)).astype(BF16)
        return going_right.astype(F32) + going_left.astype(F32) + term(0)

    def exchange(blocks):
        return lax.all_to_all(blocks, "shard", split_axis=0, concat_axis=0, tiled=True)

    def pick(array, index, axis):
        return lax.dynamic_index_in_dim(array, index, axis, keepdims=False)

    def add(a, b):
        return (a.astype(F32) + b.astype(F32)).astype(BF16)

    def rep_pieces(piece):
        mine = lax.axis_index("rep")
        far = (mine + 2) % rep
        other_chip = chip_swap(piece)
        other_core = core_swap(piece)
        last = core_swap(other_chip)
        return [(mine, piece), (mine ^ 1, other_core), (far, other_chip), (far ^ 1, last)]

    def gather_rep(piece, axis, pieces=None):
        whole = empty(piece.shape[:axis] + (rep,) + piece.shape[axis:], piece.dtype)
        for index, part in rep_pieces(piece) if pieces is None else pieces:
            whole = lax.dynamic_update_index_in_dim(whole, part, index, axis)
        return whole

    def scatter_rep(blocks):
        mine = lax.axis_index("rep")
        chip, core = mine // 2, mine % 2
        blocks = blocks.reshape((blocks.shape[0], outer, 2) + blocks.shape[2:])
        half = add(pick(blocks, core, 2), core_swap(pick(blocks, 1 - core, 2)))
        return add(pick(half, chip, 1), chip_swap(pick(half, 1 - chip, 1)))

    def local(
        tokens,
        doc_lengths,
        pic_starts,
        attn_gain,
        w_query,
        w_key,
        w_value,
        w_out,
        ffn_gain,
        w_gate,
        w_up,
        w_down,
        cotangent,
    ):
        rows, width = tokens.shape
        heads = width // HD
        base = heads // n
        slots = -(-heads // n)
        block = slots * HD
        main = base * HD
        mains = n * main
        over = heads - n * base
        depth = w_query.shape[0]
        part = depth // rep
        ff = w_gate.shape[1]
        cols = ff // n
        all_rows = n * rows
        me = lax.axis_index("shard")
        mine = lax.axis_index("rep")
        own = mine.reshape(1)
        docs = doc_lengths.shape[1]
        pics = pic_starts.shape[1]

        def by_rep(array):
            return array.reshape(rep, -1, array.shape[1])

        gain_one = by_rep(low(attn_gain)[:, None])
        gain_two = by_rep(low(ffn_gain)[:, None])

        def by_heads(array):
            first = array[:mains].reshape(n, main, -1)
            if slots == base:
                return first
            rest = jnp.pad(array[mains:], ((0, n * HD - (width - mains)), (0, 0)))
            return jnp.concatenate([first, rest.reshape(n, HD, -1)], axis=1)

        def from_heads(array, kind):
            first = array[:, :, kind * main : (kind + 1) * main].transpose(1, 0, 2)
            first = first.reshape(array.shape[1], mains)
            if slots == base:
                return first
            start = 3 * main + kind * HD
            rest = array[:over, :, start : start + HD].transpose(1, 0, 2)
            return jnp.concatenate([first, rest.reshape(array.shape[1], width - mains)], axis=1)

        info = jnp.concatenate([doc_lengths[0], pic_starts[0]]).astype(BF16)
        info = jnp.zeros((8, 3 * block), BF16).at[0, : docs + pics].set(info)
        qkv_part = prepare(
            functools.partial(prepare_kernel, n, base, slots, heads),
            own,
            [by_rep(w) for w in (w_query, w_key, w_value)],
            gain_one,
            [info],
            (n, part + 8, 3 * block),
            "prepare_qkv",
        )
        ffn_part = prepare(
            functools.partial(prepare_ffn_kernel, n),
            own,
            [by_rep(w) for w in (w_gate, w_up)],
            gain_two,
            [],
            (n, 2 * part, cols),
            "prepare_ffn",
        )
        qkv_part = exchange(qkv_part)
        x_pieces = ring_gather(tokens, (None, (qkv_part, ffn_part)), True)
        info = qkv_part[:, part, : docs + pics].astype(jnp.int32)
        near = x_pieces[-2][1]
        out_part = pick(by_rep(w_out), mine, 0).astype(BF16)
        out_w = lax.all_gather(out_part, ("shard", "rep"), axis=0, tiled=True)
        ffn_part = exchange(after(ffn_part, near))
        qkv_part = qkv_part[:, :part]
        last, qkv_chip = lax.optimization_barrier((x_pieces[-1][1], chip_swap(qkv_part)))
        x_pieces[-1] = (x_pieces[-1][0], last)
        inputs = assemble(x_pieces)
        far = (mine + 2) % rep
        qkv_pieces = [
            (mine, qkv_part),
            (mine ^ 1, core_swap(qkv_part)),
            (far, qkv_chip),
            (far ^ 1, core_swap(qkv_chip)),
        ]
        qkv_w = gather_rep(qkv_part, 1, qkv_pieces).reshape(width, 3 * block)
        down_w = w_down.astype(BF16)
        grad_result = cotangent.astype(F32)

        offsets, allowed = jax.vmap(lambda a, b: layout(a, b, rows))(info[:, :docs], info[:, docs:])
        bias = jnp.where(allowed, 0.0, MASKED).astype(F32)
        freq_table = jnp.exp(jnp.arange(HALF, dtype=F32) * (-2.0 * math.log(10000.0) / HD))
        turned = freq_table[:, None] * offsets.reshape(1, all_rows).astype(F32)
        cosine, sine = jnp.cos(turned), jnp.sin(turned)
        squares = jnp.mean(jnp.square(inputs.astype(F32)), axis=-1)
        scale_one = lax.rsqrt(squares + EPSILON)[None, :]
        qkv = mm(qkv_w, inputs, 0, 1)
        qkv, mixed = attend(base, slots, n, rows, qkv, scale_one, cosine, sine, bias)
        ffn_part = after(ffn_part, mixed)
        ffn_pieces = rep_pieces(ffn_part)
        gate_w, up_w = (
            gather_rep(
                ffn_part[:, k * part : (k + 1) * part],
                1,
                [(at, piece[:, k * part : (k + 1) * part]) for at, piece in ffn_pieces],
            ).reshape(width, cols)
            for k in range(2)
        )
        mixed_all = empty((n * block, all_rows), BF16)
        mixed_pieces = ring_gather(mixed, (), True)
        for device, piece in mixed_pieces:
            mixed_all = lax.dynamic_update_slice_in_dim(mixed_all, piece[:main], device * main, 0)
            if slots > base:
                mixed_all = lax.dynamic_update_slice_in_dim(
                    mixed_all, piece[main:], mains + device * HD, 0
                )
        middle_low, scale_two, my_middle = middle_rows(me, mixed_all, out_w, inputs, rows)

        gate_act = mm(middle_low, gate_w, 1, 0) * scale_two
        up_act = mm(middle_low, up_w, 1, 0) * scale_two
        sigmoid_gate = jax.nn.sigmoid(gate_act)
        silu_gate = gate_act * sigmoid_gate
        inner = (silu_gate * up_act).astype(BF16)
        grad_branch = (BRANCH_SCALE * grad_result).astype(BF16)
        grad_branch = assemble(ring_gather(grad_branch, (mixed_pieces[-1][1], scale_two, up_act)))
        grad_inner = mm(grad_branch, down_w, 1, 1)
        grad_gate_act = (
            grad_inner
            * up_act
            * sigmoid_gate
            * (1.0 + gate_act * (1.0 - sigmoid_gate))
            * scale_two
        ).astype(BF16)
        grad_up_act = (grad_inner * silu_gate * scale_two).astype(BF16)
        partial = mm(grad_gate_act, gate_w, 1, 1) + mm(grad_up_act, up_w, 1, 1)
        partial = partial.astype(BF16).reshape(n, rows, width)
        back_two = scatter_shard(partial)
        my_normed_two = my_middle * lax.dynamic_slice_in_dim(scale_two, me * rows, rows, 0)
        inner_mean = jnp.mean(back_two * my_normed_two, axis=-1, keepdims=True)
        grad_middle = grad_result + back_two - my_normed_two * inner_mean

        def rep_rows(grad):
            return row_major(grad.astype(BF16)).reshape(n, rep, part, grad.shape[1])

        def finish_some(pieces, weights, gain, done):
            for index, arrived in pieces:
                done = finish(
                    arrived, index.reshape(1), rep, [by_rep(w) for w in weights], gain, done
                )
            return done

        def finish_all(piece, weights, gain):
            done = finish_some(rep_pieces(piece), weights, gain, None)
            return [a.reshape(-1, a.shape[2]) for a in done]

        inner, grad_gate_act, grad_up_act, _ = lax.optimization_barrier(
            (inner, grad_gate_act, grad_up_act, partial)
        )
        grad_down = mm(inner, grad_branch, 0, 0).astype(BF16).reshape(1, rep, -1, width)
        (grad_down,) = finish_all(scatter_rep(grad_down), (), None)
        grad_ffn = [rep_rows(mm(middle_low, g, 0, 0)) for g in (grad_gate_act, grad_up_act)]
        grad_ffn = scatter_rep(jnp.concatenate(grad_ffn, axis=2))
        grad_attn = (BRANCH_SCALE * grad_middle).astype(BF16)
        both = exchange(
            jnp.concatenate(
                [
                    by_heads(mm(out_w, grad_attn, 1, 1).astype(BF16)),
                    grad_attn.T.reshape(n, depth, rows),
                ],
                axis=1,
            )
        )
        grad_mixed = both[:, :block].transpose(1, 0, 2).reshape(block, all_rows)
        grad_attn_cols = both[:, block:].transpose(1, 0, 2).reshape(depth, all_rows)
        grad_qkv = attend_back(
            base, slots, n, rows, qkv, grad_mixed, scale_one, cosine, sine, bias
        )
        grad_w = jnp.concatenate(
            [
                row_major(mm(inputs, grad_qkv, 0, 1).astype(BF16)),
                row_major(mm(mixed_all, after(grad_attn_cols, grad_qkv), 1, 1).astype(BF16))[:width],
            ],
            axis=1,
        )
        grad_w, grad_ffn = lax.optimization_barrier((grad_w, grad_ffn))
        grad_ffn = exchange(grad_ffn)
        partial = mm(after(grad_qkv, grad_w), qkv_w, 0, 1)
        ffn_blocks = grad_ffn
        grad_ffn = grad_ffn.reshape(n, 2, part, cols).transpose(1, 2, 0, 3).reshape(2, part, ff)
        back_one = scatter_shard(
            partial.astype(BF16).reshape(n, rows, width), (None, None, ffn_blocks)
        )
        ffn_pieces = rep_pieces(grad_ffn)
        ffn_half = finish_some(ffn_pieces[:2], (w_gate, w_up), gain_two, None)
        ffn_done = finish_some(ffn_pieces[2:], (w_gate, w_up), gain_two, ffn_half)
        grad_gate, grad_up, grad_gain_two = (a.reshape(-1, a.shape[2]) for a in ffn_done)
        my_inputs = tokens.astype(F32)
        my_scale_one = lax.rsqrt(jnp.mean(my_inputs * my_inputs, axis=-1, keepdims=True) + EPSILON)
        my_normed_one = my_inputs * my_scale_one
        inner_mean = jnp.mean(back_one * my_normed_one, axis=-1, keepdims=True)
        input_grad = grad_middle + back_one - my_normed_one * inner_mean

        branch = mm(after(inner, back_two), down_w, 1, 0).astype(BF16).reshape(n, rows, width)
        branch = scatter_shard(after(branch, back_one), (None, grad_down, None, ffn_half))
        out_tokens = (my_middle + BRANCH_SCALE * branch).astype(BF16)

        grad_w = exchange(scatter_rep(grad_w.reshape(n, rep, part, -1)))
        grad_w = jnp.stack(
            [from_heads(grad_w, kind) for kind in range(3)]
            + [grad_w[:, :, 3 * block :].transpose(1, 0, 2).reshape(part, width)]
        )
        grad_query, grad_key, grad_value, grad_out, grad_gain_one = finish_all(
            grad_w, (w_query, w_key, w_value), gain_one
        )
        return (
            out_tokens,
            input_grad,
            grad_gain_one.reshape(depth),
            grad_query,
            grad_key,
            grad_value,
            grad_out,
            grad_gain_two.reshape(depth),
            grad_gate,
            grad_up,
            grad_down,
        )

    return local


def solution(mesh):
    tokens = P(("rep", "shard"), None)
    weight = P("shard", None)
    gain = P("shard")
    return jax.shard_map(
        build(mesh.shape["rep"], mesh.shape["shard"]),
        mesh=mesh,
        in_specs=(
            tokens,
            tokens,
            tokens,
            gain,
            weight,
            weight,
            weight,
            weight,
            gain,
            weight,
            weight,
            weight,
            tokens,
        ),
        out_specs=(
            tokens,
            tokens,
            gain,
            weight,
            weight,
            weight,
            weight,
            gain,
            weight,
            weight,
            weight,
        ),
        check_vma=False,
    )
```

```python
import functools
import math

import jax
import jax.numpy as jnp
from jax import lax
from jax.experimental import pallas as pl
from jax.experimental.layout import Layout, with_layout_constraint
from jax.experimental.pallas import tpu as pltpu
from jax.sharding import PartitionSpec as P

HD = 64
HALF = HD // 2
PIC = 64

EPSILON = 1e-05
BRANCH_SCALE = 1.4 / math.sqrt(40.0)
MASKED = -1e30
F32 = jnp.float32
BF16 = jnp.bfloat16


def mm(left, right, left_dim, right_dim):
    return lax.dot_general(
        left, right, (((left_dim,), (right_dim,)), ((), ())), preferred_element_type=F32
    )


def layout(lengths, starts, row_count):
    places = jnp.arange(row_count, dtype=jnp.int32)
    bounds = jnp.cumsum(lengths)
    firsts = bounds - lengths
    member = (places[:, None] >= firsts[None, :]) & (places[:, None] < bounds[None, :])
    doc_of = jnp.sum(
        jnp.where(member, jnp.arange(lengths.shape[0], dtype=jnp.int32)[None, :], 0), axis=1
    )
    starting = jnp.sum(jnp.where(member, firsts[None, :], 0), axis=1)
    inside = (places[None, :] >= starts[:, None]) & (places[None, :] < starts[:, None] + PIC)
    shared = jnp.any(inside[:, :, None] & inside[:, None, :], axis=0)
    causal = places[None, :] >= places[:, None]
    allowed = (doc_of[:, None] == doc_of[None, :]) & (causal | shared)
    return (places - starting, allowed)


def turn(values, cosine, sine):
    first, second = values[:HALF], values[HALF:]
    return jnp.concatenate([first * cosine - second * sine, second * cosine + first * sine], axis=0)


def probabilities(keys, query, bias):
    scores = mm(keys, query, 0, 0) * HD**-0.5 + bias
    expo = jnp.exp(scores - jnp.max(scores, axis=0, keepdims=True))
    return expo * (1.0 / jnp.sum(expo, axis=0, keepdims=True))


def feature_rows(base, slots, kind, head):
    if head < base:
        return (kind * base + head) * HD
    return (3 * base + kind * (slots - base) + head - base) * HD


def attend_kernel(base, slots, qkv_ref, scale_ref, cos_ref, sin_ref, bias_ref, qkv_out_ref, mixed_ref):
    scale = scale_ref[...]
    cosine, sine, bias = cos_ref[...], sin_ref[...], bias_ref[0]
    for head in range(slots):
        at = [pl.ds(feature_rows(base, slots, kind, head), HD) for kind in range(3)]
        query = turn(qkv_ref[at[0], :] * scale, cosine, sine).astype(BF16)
        keys = turn(qkv_ref[at[1], :] * scale, cosine, sine).astype(BF16)
        values = (qkv_ref[at[2], :] * scale).astype(BF16)
        qkv_out_ref[at[0], :] = query
        qkv_out_ref[at[1], :] = keys
        qkv_out_ref[at[2], :] = values
        probs = probabilities(keys, query, bias).astype(BF16)
        mixed_ref[pl.ds(head * HD, HD), :] = mm(values, probs, 1, 0).astype(BF16)


def attend_back_kernel(base, slots, qkv_ref, grad_ref, scale_ref, cos_ref, sin_ref, bias_ref, out_ref):
    scale = scale_ref[...]
    cosine, sine, bias = cos_ref[...], sin_ref[...], bias_ref[0]
    back = scale * HD**-0.5
    for head in range(slots):
        at = [pl.ds(feature_rows(base, slots, kind, head), HD) for kind in range(3)]
        query = qkv_ref[at[0], :]
        keys = qkv_ref[at[1], :]
        values = qkv_ref[at[2], :]
        grad = grad_ref[pl.ds(head * HD, HD), :]
        probs = probabilities(keys, query, bias)
        grad_values = mm(grad, probs.astype(BF16), 1, 1)
        grad_probs = mm(values, grad, 0, 0)
        inner = jnp.sum(probs * grad_probs, axis=0, keepdims=True)
        grad_scores = (probs * (grad_probs - inner)).astype(BF16)
        grad_query = turn(mm(keys, grad_scores, 1, 0) * back, cosine, -sine)
        grad_keys = turn(mm(query, grad_scores, 1, 1) * back, cosine, -sine)
        out_ref[at[0], :] = grad_query.astype(BF16)
        out_ref[at[1], :] = grad_keys.astype(BF16)
        out_ref[at[2], :] = (grad_values * scale).astype(BF16)


def columns(height, rows):
    return pl.BlockSpec((height, rows), lambda r: (0, r))


def attention_specs(rows):
    return [
        columns(1, rows),
        columns(HALF, rows),
        columns(HALF, rows),
        pl.BlockSpec((1, rows, rows), lambda r: (r, 0, 0)),
    ]


def attend(base, slots, n, rows, qkv, scale, cosine, sine, bias):
    block = slots * HD
    tokens = n * rows
    flops = 4 * n * slots * rows * rows * HD
    return pl.pallas_call(
        functools.partial(attend_kernel, base, slots),
        grid=(n,),
        in_specs=[columns(3 * block, rows)] + attention_specs(rows),
        out_specs=[columns(3 * block, rows), columns(block, rows)],
        out_shape=[
            jax.ShapeDtypeStruct((3 * block, tokens), BF16),
            jax.ShapeDtypeStruct((block, tokens), BF16),
        ],
        cost_estimate=pl.CostEstimate(
            flops=flops, bytes_accessed=20 * block * tokens, transcendentals=n * slots * rows * rows
        ),
        compiler_params=pltpu.CompilerParams(vmem_limit_bytes=12 * 2**20),
        name="attend",
    )(qkv, scale, cosine, sine, bias)


def attend_back(base, slots, n, rows, qkv, grad, scale, cosine, sine, bias):
    block = slots * HD
    tokens = n * rows
    flops = 10 * n * slots * rows * rows * HD
    return pl.pallas_call(
        functools.partial(attend_back_kernel, base, slots),
        grid=(n,),
        in_specs=[columns(3 * block, rows), columns(block, rows)] + attention_specs(rows),
        out_specs=columns(3 * block, rows),
        out_shape=jax.ShapeDtypeStruct((3 * block, tokens), BF16),
        cost_estimate=pl.CostEstimate(
            flops=flops, bytes_accessed=14 * block * tokens, transcendentals=n * slots * rows * rows
        ),
        compiler_params=pltpu.CompilerParams(vmem_limit_bytes=16 * 2**20),
        name="attend_back",
    )(qkv, grad, scale, cosine, sine, bias)


def middle_kernel(me_ref, mixed_ref, weight_ref, inputs_ref, low_ref, scale_ref, own_ref):
    branch = mm(mixed_ref[...], weight_ref[...], 0, 0)
    middle = inputs_ref[...].astype(F32) + BRANCH_SCALE * branch
    scale = lax.rsqrt(jnp.mean(middle * middle, axis=1, keepdims=True) + EPSILON)
    low_ref[...] = middle.astype(BF16)
    scale_ref[...] = scale

    @pl.when(pl.program_id(0) == me_ref[0])
    def _():
        own_ref[...] = middle


def middle_rows(me, mixed, weight, inputs, rows):
    tokens, width = inputs.shape
    return pl.pallas_call(
        middle_kernel,
        grid_spec=pltpu.PrefetchScalarGridSpec(
            num_scalar_prefetch=1,
            grid=(tokens // rows,),
            in_specs=[
                pl.BlockSpec((width, rows), lambda i, me: (0, i)),
                pl.BlockSpec((width, width), lambda i, me: (0, 0), pipeline_mode=pl.Buffered(1)),
                pl.BlockSpec((rows, width), lambda i, me: (i, 0)),
            ],
            out_specs=[
                pl.BlockSpec((rows, width), lambda i, me: (i, 0)),
                pl.BlockSpec((rows, 1), lambda i, me: (i, 0)),
                pl.BlockSpec((rows, width), lambda i, me: (0, 0)),
            ],
        ),
        out_shape=[
            jax.ShapeDtypeStruct((tokens, width), BF16),
            jax.ShapeDtypeStruct((tokens, 1), F32),
            jax.ShapeDtypeStruct((rows, width), F32),
        ],
        cost_estimate=pl.CostEstimate(
            flops=2 * tokens * width * width,
            bytes_accessed=2 * width * width + 6 * tokens * width,
            transcendentals=tokens,
        ),
        compiler_params=pltpu.CompilerParams(vmem_limit_bytes=40 * 2**20),
        name="middle_rows",
    )(me.reshape(1), mixed, weight, inputs)


def row_major(array):
    return with_layout_constraint(array, Layout(tuple(range(array.ndim))))


def empty(shape, dtype):
    return pl.pallas_call(
        lambda out_ref: None,
        out_specs=pl.BlockSpec(memory_space=pl.ANY),
        out_shape=jax.ShapeDtypeStruct(shape, dtype),
        compiler_params=pltpu.CompilerParams(vmem_limit_bytes=1 * 2**20),
        name="empty",
    )()


def low(weight):
    return weight.astype(BF16).astype(F32)


def prepare_kernel(n, base, slots, heads, own_ref, query_ref, key_ref, value_ref, gain_ref, info_ref, out_ref):
    part = query_ref.shape[1]
    main = base * HD
    for kind, ref in enumerate((query_ref, key_ref, value_ref)):
        weight = (low(ref[0]) * gain_ref[0]).astype(BF16)
        for j in range(n):
            out_ref[j, :part, kind * main : (kind + 1) * main] = weight[:, j * main : (j + 1) * main]
            if slots > base:
                first = 3 * main + kind * HD
                head = n * base + j
                if head < heads:
                    extra = weight[:, head * HD : (head + 1) * HD]
                else:
                    extra = jnp.zeros((part, HD), BF16)
                out_ref[j, :part, first : first + HD] = extra
    for j in range(n):
        out_ref[j, part:, :] = info_ref[...]


def prepare_ffn_kernel(n, own_ref, gate_ref, up_ref, gain_ref, out_ref):
    part, cols = gate_ref.shape[1], out_ref.shape[2]
    for kind, ref in enumerate((gate_ref, up_ref)):
        weight = (low(ref[0]) * gain_ref[0]).astype(BF16)
        for j in range(n):
            out_ref[j, kind * part : (kind + 1) * part, :] = weight[:, j * cols : (j + 1) * cols]


def own_part(part, width):
    return pl.BlockSpec((1, part, width), lambda i, own: (own[0], 0, 0))


def prepare(kernel, own, weights, gain, more, out_shape, name):
    part = weights[0].shape[1]
    return pl.pallas_call(
        kernel,
        grid_spec=pltpu.PrefetchScalarGridSpec(
            num_scalar_prefetch=1,
            grid=(1,),
            in_specs=[own_part(part, w.shape[2]) for w in weights]
            + [own_part(part, 1)]
            + [pl.BlockSpec(m.shape, lambda i, own: (0, 0)) for m in more],
            out_specs=pl.BlockSpec(out_shape, lambda i, own: (0, 0, 0)),
        ),
        out_shape=jax.ShapeDtypeStruct(out_shape, BF16),
        name=name,
    )(own, *weights, gain, *more)


def finish_kernel(count, gained, at_ref, piece_ref, *refs):
    weights = refs[:gained]
    outs = refs[-(count + (gained > 0)) :]
    total = 0.0
    for k in range(count):
        raw = piece_ref[k].astype(F32)
        if k < gained:
            total = total + jnp.sum(weights[k][0] * raw, axis=1, keepdims=True)
            raw = raw * refs[gained][0]
        outs[k][0] = raw
    if gained:
        first = pl.program_id(0) == 0
        outs[count][0] = jnp.where(first, 0.0, outs[count][0]) + total


def finish(piece, at, rep, weights, gain, previous):
    count, part, width = piece.shape
    gained = len(weights)
    chunk = 1152 if width == 2304 else width

    def placed(size, moving):
        return pl.BlockSpec((1, part, size), lambda i, at: (at[0], 0, i if moving else 0))

    in_specs = [pl.BlockSpec((count, part, chunk), lambda i, at: (0, 0, i))]
    operands = [piece]
    out_specs = [placed(chunk, True)] * count
    out_shape = [jax.ShapeDtypeStruct((rep, part, width), F32)] * count
    if gained:
        in_specs += [placed(chunk, True)] * gained + [placed(1, False)]
        operands += list(weights) + [gain]
        out_specs.append(placed(1, False))
        out_shape.append(jax.ShapeDtypeStruct((rep, part, 1), F32))
    aliases = {}
    if previous is not None:
        aliases = {1 + len(operands) + k: k for k in range(len(out_shape))}
        operands += list(previous)
        in_specs += [pl.BlockSpec(memory_space=pl.ANY)] * len(out_shape)
    return pl.pallas_call(
        functools.partial(finish_kernel, count, gained),
        grid_spec=pltpu.PrefetchScalarGridSpec(
            num_scalar_prefetch=1, grid=(width // chunk,), in_specs=in_specs, out_specs=out_specs
        ),
        out_shape=out_shape,
        input_output_aliases=aliases,
        cost_estimate=pl.CostEstimate(
            flops=4 * count * part * width,
            bytes_accessed=(6 * count + 4 * gained) * part * width,
            transcendentals=0,
        ),
        name="finish",
    )(at, *operands)


def build(rep, n):
    cycle = list(range(0, n, 2)) + list(range(n - 1, 0, -2)) if n % 2 == 0 else list(range(n))
    to_right = [(cycle[i], cycle[(i + 1) % n]) for i in range(n)]
    to_left = [(b, a) for a, b in to_right]
    steps_right = n // 2
    steps_left = n - 1 - steps_right
    outer = rep // 2
    core_pairs = [(i, i ^ 1) for i in range(rep)]
    chip_pairs = [(i, (i + 2) % rep) for i in range(rep)]

    def right(x):
        return lax.ppermute(x, "shard", to_right)

    def left(x):
        return lax.ppermute(x, "shard", to_left)

    def core_swap(x):
        return lax.ppermute(x, "rep", core_pairs)

    def chip_swap(x):
        return lax.ppermute(x, "rep", chip_pairs)

    def ring_device(offset):
        device = lax.axis_index("shard")
        if n % 2:
            return (device + offset + n) % n
        place = jnp.where(device % 2 == 0, device // 2, n - 1 - device // 2)
        place = (place + offset + n) % n
        return jnp.where(place < n // 2, 2 * place, 2 * (n - 1 - place) + 1)

    def after(value, *others):
        return lax.optimization_barrier((value, others))[0]

    def ring_gather(piece, gates=(), paired=False):
        pieces = [(ring_device(0), piece)]
        going_right = going_left = piece
        for step in range(1, steps_right + 1):
            if step <= len(gates) and gates[step - 1] is not None:
                going_right, going_left = after((going_right, going_left), gates[step - 1])
            going_right = right(going_right)
            if step <= steps_left:
                going_left = left(going_left)
                if paired:
                    going_right, going_left = lax.optimization_barrier((going_right, going_left))
                pieces.append((ring_device(step), going_left))
            pieces.append((ring_device(-step), going_right))
        return pieces

    def assemble(pieces):
        shape = pieces[0][1].shape
        whole = empty((n,) + shape, pieces[0][1].dtype)
        for device, part in pieces:
            whole = lax.dynamic_update_index_in_dim(whole, part, device, 0)
        return whole.reshape((-1,) + shape[1:])

    def scatter_shard(parts, gates=()):
        def term(offset):
            return lax.dynamic_index_in_dim(parts, ring_device(offset), 0, keepdims=False).astype(F32)

        going_right = term(steps_right).astype(BF16)
        going_left = term(-steps_left).astype(BF16)
        for step in range(1, steps_right + 1):
            if step <= len(gates) and gates[step - 1] is not None:
                going_right, going_left = after((going_right, going_left), gates[step - 1])
            going_right = right(going_right)
            if step < steps_right:
                going_right = (going_right.astype(F32) + term(steps_right - step)).astype(BF16)
            if step <= steps_left:
                going_left = left(going_left)
                if step < steps_left:
                    going_left = (going_left.astype(F32) + term(step - steps_left)).astype(BF16)
        return going_right.astype(F32) + going_left.astype(F32) + term(0)

    def exchange(blocks):
        return lax.all_to_all(blocks, "shard", split_axis=0, concat_axis=0, tiled=True)

    def pick(array, index, axis):
        return lax.dynamic_index_in_dim(array, index, axis, keepdims=False)

    def add(a, b):
        return (a.astype(F32) + b.astype(F32)).astype(BF16)

    def rep_pieces(piece):
        mine = lax.axis_index("rep")
        far = (mine + 2) % rep
        other_chip = chip_swap(piece)
        other_core = core_swap(piece)
        last = core_swap(other_chip)
        return [(mine, piece), (mine ^ 1, other_core), (far, other_chip), (far ^ 1, last)]

    def gather_rep(piece, axis, pieces=None):
        whole = empty(piece.shape[:axis] + (rep,) + piece.shape[axis:], piece.dtype)
        for index, part in rep_pieces(piece) if pieces is None else pieces:
            whole = lax.dynamic_update_index_in_dim(whole, part, index, axis)
        return whole

    def scatter_rep(blocks):
        mine = lax.axis_index("rep")
        chip, core = mine // 2, mine % 2
        blocks = blocks.reshape((blocks.shape[0], outer, 2) + blocks.shape[2:])
        half = add(pick(blocks, core, 2), core_swap(pick(blocks, 1 - core, 2)))
        return add(pick(half, chip, 1), chip_swap(pick(half, 1 - chip, 1)))

    def local(
        tokens,
        doc_lengths,
        pic_starts,
        attn_gain,
        w_query,
        w_key,
        w_value,
        w_out,
        ffn_gain,
        w_gate,
        w_up,
        w_down,
        cotangent,
    ):
        rows, width = tokens.shape
        heads = width // HD
        base = heads // n
        slots = -(-heads // n)
        block = slots * HD
        main = base * HD
        mains = n * main
        over = heads - n * base
        depth = w_query.shape[0]
        part = depth // rep
        ff = w_gate.shape[1]
        cols = ff // n
        all_rows = n * rows
        me = lax.axis_index("shard")
        mine = lax.axis_index("rep")
        own = mine.reshape(1)
        docs = doc_lengths.shape[1]
        pics = pic_starts.shape[1]

        def by_rep(array):
            return array.reshape(rep, -1, array.shape[1])

        gain_one = by_rep(low(attn_gain)[:, None])
        gain_two = by_rep(low(ffn_gain)[:, None])

        def by_heads(array):
            first = array[:mains].reshape(n, main, -1)
            if slots == base:
                return first
            rest = jnp.pad(array[mains:], ((0, n * HD - (width - mains)), (0, 0)))
            return jnp.concatenate([first, rest.reshape(n, HD, -1)], axis=1)

        def from_heads(array, kind):
            first = array[:, :, kind * main : (kind + 1) * main].transpose(1, 0, 2)
            first = first.reshape(array.shape[1], mains)
            if slots == base:
                return first
            start = 3 * main + kind * HD
            rest = array[:over, :, start : start + HD].transpose(1, 0, 2)
            return jnp.concatenate([first, rest.reshape(array.shape[1], width - mains)], axis=1)

        info = jnp.concatenate([doc_lengths[0], pic_starts[0]]).astype(BF16)
        info = jnp.zeros((8, 3 * block), BF16).at[0, : docs + pics].set(info)
        qkv_part = prepare(
            functools.partial(prepare_kernel, n, base, slots, heads),
            own,
            [by_rep(w) for w in (w_query, w_key, w_value)],
            gain_one,
            [info],
            (n, part + 8, 3 * block),
            "prepare_qkv",
        )
        ffn_part = prepare(
            functools.partial(prepare_ffn_kernel, n),
            own,
            [by_rep(w) for w in (w_gate, w_up)],
            gain_two,
            [],
            (n, 2 * part, cols),
            "prepare_ffn",
        )
        qkv_part = exchange(qkv_part)
        x_pieces = ring_gather(tokens, (None, (qkv_part, ffn_part)), True)
        info = qkv_part[:, part, : docs + pics].astype(jnp.int32)
        near = x_pieces[-2][1]
        out_part = pick(by_rep(w_out), mine, 0).astype(BF16)
        out_w = lax.all_gather(out_part, ("shard", "rep"), axis=0, tiled=True)
        ffn_part = exchange(after(ffn_part, near))
        qkv_part = qkv_part[:, :part]
        last, qkv_chip = lax.optimization_barrier((x_pieces[-1][1], chip_swap(qkv_part)))
        x_pieces[-1] = (x_pieces[-1][0], last)
        inputs = assemble(x_pieces)
        far = (mine + 2) % rep
        qkv_pieces = [
            (mine, qkv_part),
            (mine ^ 1, core_swap(qkv_part)),
            (far, qkv_chip),
            (far ^ 1, core_swap(qkv_chip)),
        ]
        qkv_w = gather_rep(qkv_part, 1, qkv_pieces).reshape(width, 3 * block)
        down_w = w_down.astype(BF16)
        grad_result = cotangent.astype(F32)

        offsets, allowed = jax.vmap(lambda a, b: layout(a, b, rows))(info[:, :docs], info[:, docs:])
        bias = jnp.where(allowed, 0.0, MASKED).astype(F32)
        freq_table = jnp.exp(jnp.arange(HALF, dtype=F32) * (-2.0 * math.log(10000.0) / HD))
        turned = freq_table[:, None] * offsets.reshape(1, all_rows).astype(F32)
        cosine, sine = jnp.cos(turned), jnp.sin(turned)
        squares = jnp.mean(jnp.square(inputs.astype(F32)), axis=-1)
        scale_one = lax.rsqrt(squares + EPSILON)[None, :]
        qkv = mm(qkv_w, inputs, 0, 1)
        qkv, mixed = attend(base, slots, n, rows, qkv, scale_one, cosine, sine, bias)
        ffn_part = after(ffn_part, mixed)
        ffn_pieces = rep_pieces(ffn_part)
        gate_w, up_w = (
            gather_rep(
                ffn_part[:, k * part : (k + 1) * part],
                1,
                [(at, piece[:, k * part : (k + 1) * part]) for at, piece in ffn_pieces],
            ).reshape(width, cols)
            for k in range(2)
        )
        mixed_all = empty((n * block, all_rows), BF16)
        mixed_pieces = ring_gather(mixed, (), True)
        for device, piece in mixed_pieces:
            mixed_all = lax.dynamic_update_slice_in_dim(mixed_all, piece[:main], device * main, 0)
            if slots > base:
                mixed_all = lax.dynamic_update_slice_in_dim(
                    mixed_all, piece[main:], mains + device * HD, 0
                )
        middle_low, scale_two, my_middle = middle_rows(me, mixed_all, out_w, inputs, rows)

        gate_act = mm(middle_low, gate_w, 1, 0) * scale_two
        up_act = mm(middle_low, up_w, 1, 0) * scale_two
        sigmoid_gate = jax.nn.sigmoid(gate_act)
        silu_gate = gate_act * sigmoid_gate
        inner = (silu_gate * up_act).astype(BF16)
        grad_branch = (BRANCH_SCALE * grad_result).astype(BF16)
        grad_branch = assemble(ring_gather(grad_branch, (mixed_pieces[-1][1], scale_two, up_act)))
        grad_inner = mm(grad_branch, down_w, 1, 1)
        grad_gate_act = (
            grad_inner
            * up_act
            * sigmoid_gate
            * (1.0 + gate_act * (1.0 - sigmoid_gate))
            * scale_two
        ).astype(BF16)
        grad_up_act = (grad_inner * silu_gate * scale_two).astype(BF16)
        partial = mm(grad_gate_act, gate_w, 1, 1) + mm(grad_up_act, up_w, 1, 1)
        partial = partial.astype(BF16).reshape(n, rows, width)
        back_two = scatter_shard(partial)
        my_normed_two = my_middle * lax.dynamic_slice_in_dim(scale_two, me * rows, rows, 0)
        inner_mean = jnp.mean(back_two * my_normed_two, axis=-1, keepdims=True)
        grad_middle = grad_result + back_two - my_normed_two * inner_mean

        def rep_rows(grad):
            return row_major(grad.astype(BF16)).reshape(n, rep, part, grad.shape[1])

        def finish_some(pieces, weights, gain, done):
            for index, arrived in pieces:
                done = finish(
                    arrived, index.reshape(1), rep, [by_rep(w) for w in weights], gain, done
                )
            return done

        def finish_all(piece, weights, gain):
            done = finish_some(rep_pieces(piece), weights, gain, None)
            return [a.reshape(-1, a.shape[2]) for a in done]

        inner, grad_gate_act, grad_up_act, _ = lax.optimization_barrier(
            (inner, grad_gate_act, grad_up_act, partial)
        )
        grad_down = mm(inner, grad_branch, 0, 0).astype(BF16).reshape(1, rep, -1, width)
        (grad_down,) = finish_all(scatter_rep(grad_down), (), None)
        grad_ffn = [rep_rows(mm(middle_low, g, 0, 0)) for g in (grad_gate_act, grad_up_act)]
        grad_ffn = scatter_rep(jnp.concatenate(grad_ffn, axis=2))
        grad_attn = (BRANCH_SCALE * grad_middle).astype(BF16)
        both = exchange(
            jnp.concatenate(
                [
                    by_heads(mm(out_w, grad_attn, 1, 1).astype(BF16)),
                    grad_attn.T.reshape(n, depth, rows),
                ],
                axis=1,
            )
        )
        grad_mixed = both[:, :block].transpose(1, 0, 2).reshape(block, all_rows)
        grad_attn_cols = both[:, block:].transpose(1, 0, 2).reshape(depth, all_rows)
        grad_qkv = attend_back(
            base, slots, n, rows, qkv, grad_mixed, scale_one, cosine, sine, bias
        )
        grad_w = jnp.concatenate(
            [
                row_major(mm(inputs, grad_qkv, 0, 1).astype(BF16)),
                row_major(mm(mixed_all, after(grad_attn_cols, grad_qkv), 1, 1).astype(BF16))[:width],
            ],
            axis=1,
        )
        grad_w, grad_ffn = lax.optimization_barrier((grad_w, grad_ffn))
        grad_ffn = exchange(grad_ffn)
        partial = mm(after(grad_qkv, grad_w), qkv_w, 0, 1)
        ffn_blocks = grad_ffn
        grad_ffn = grad_ffn.reshape(n, 2, part, cols).transpose(1, 2, 0, 3).reshape(2, part, ff)
        back_one = scatter_shard(
            partial.astype(BF16).reshape(n, rows, width), (None, None, ffn_blocks)
        )
        ffn_pieces = rep_pieces(grad_ffn)
        ffn_half = finish_some(ffn_pieces[:2], (w_gate, w_up), gain_two, None)
        ffn_done = finish_some(ffn_pieces[2:], (w_gate, w_up), gain_two, ffn_half)
        grad_gate, grad_up, grad_gain_two = (a.reshape(-1, a.shape[2]) for a in ffn_done)
        my_inputs = tokens.astype(F32)
        my_scale_one = lax.rsqrt(jnp.mean(my_inputs * my_inputs, axis=-1, keepdims=True) + EPSILON)
        my_normed_one = my_inputs * my_scale_one
        inner_mean = jnp.mean(back_one * my_normed_one, axis=-1, keepdims=True)
        input_grad = grad_middle + back_one - my_normed_one * inner_mean

        branch = mm(after(inner, back_two), down_w, 1, 0).astype(BF16).reshape(n, rows, width)
        branch = scatter_shard(after(branch, back_one), (None, grad_down, None, ffn_half))
        out_tokens = (my_middle + BRANCH_SCALE * branch).astype(BF16)

        grad_w = exchange(scatter_rep(grad_w.reshape(n, rep, part, -1)))
        grad_w = jnp.stack(
            [from_heads(grad_w, kind) for kind in range(3)]
            + [grad_w[:, :, 3 * block :].transpose(1, 0, 2).reshape(part, width)]
        )
        grad_query, grad_key, grad_value, grad_out, grad_gain_one = finish_all(
            grad_w, (w_query, w_key, w_value), gain_one
        )
        return (
            out_tokens,
            input_grad,
            grad_gain_one.reshape(depth),
            grad_query,
            grad_key,
            grad_value,
            grad_out,
            grad_gain_two.reshape(depth),
            grad_gate,
            grad_up,
            grad_down,
        )

    return local


def solution(mesh):
    tokens = P(("rep", "shard"), None)
    weight = P("shard", None)
    gain = P("shard")
    return jax.shard_map(
        build(mesh.shape["rep"], mesh.shape["shard"]),
        mesh=mesh,
        in_specs=(
            tokens,
            tokens,
            tokens,
            gain,
            weight,
            weight,
            weight,
            weight,
            gain,
            weight,
            weight,
            weight,
            tokens,
        ),
        out_specs=(
            tokens,
            tokens,
            gain,
            weight,
            weight,
            weight,
            weight,
            gain,
            weight,
            weight,
            weight,
        ),
        check_vma=False,
    )
```
